256 devices in a mesh: dp: 16 (over y, z_lo), expert: 16 (over z_hi, x, core).
Axes of the slice: x: 4, y: 4, z: 8 (z_hi: 2, z_lo: 4; z = z_hi * 4 + z_lo), core: 2. Of those that a mesh axis runs over, the one named last changes fastest.
Arguments:
- tokens: bfloat16 [65536, 1024], P(('dp', 'expert')), may hold values from -6 to 6
- out_grad: bfloat16 [65536, 1024], P(('dp', 'expert')), may hold values from -3 to 3
- gate_prob: bfloat16 [65536], P(('dp', 'expert')), may hold values from 0.19921875 to 1
- expert_id: int32 [65536], P(('dp', 'expert')), may hold values from 0 to 15, as said below
- up_weight: bfloat16 [16, 1024, 2048], P('expert'), may hold values from -0.1875 to 0.1875
- down_weight: bfloat16 [16, 2048, 1024], P('expert'), may hold values from -0.125 to 0.125
Outputs:
- tokens_grad: bfloat16 [65536, 1024], P(('dp', 'expert'))
- gate_grad: bfloat16 [65536], P(('dp', 'expert'))
- up_weight_grad: float32 [16, 1024, 2048], P('expert', 'dp')
- down_weight_grad: float32 [16, 2048, 1024], P('expert', 'dp')
The draws below stay inside these ranges and needn't reach their ends.
Inputs may be any that keep to these rules, and one draw needn't show every extreme that they name: `expert_id`: among the 256 tokens of one device each expert is named at most 32 times; in every data group one expert is named exactly 32 times by every device of the group.
All inputs are finite; a program needn't handle non-finite values.
Results may differ from the reference program's by a relative error of at most 0.017.
Values may be sent and summed in bfloat16 or wider, within the bound.
A program may use at most 64 MiB of HBM per device.

```python
import jax
import jax.numpy as jnp
from jax import lax

D = 1024
FF = 2048
EXP_DEV = 1
EXPERTS = 16
TOK_DEV = 256
CAP = 32
TOKENS = 65536
N_DP = 16
N_EXPERT = 16


def draw_expert_id(key, part):
    blocks = TOKENS // TOK_DEV
    group_size = EXPERTS // EXP_DEV
    groups = blocks // group_size
    remaining = TOK_DEV - CAP
    key_hot, key_blocks = jax.random.split(jax.random.fold_in(key, 17))
    hot_groups = jax.random.randint(key_hot, (groups,), 0, EXPERTS).astype(jnp.int32)
    hot_blocks = jnp.repeat(hot_groups, group_size)
    pool_offset = jnp.repeat(jnp.arange(1, EXPERTS, dtype=jnp.int32), CAP)
    block_keys = jax.random.split(key_blocks, blocks)

    def one_block(block_key, hot_expert):
        key_pool, key_rows = jax.random.split(block_key)
        shuffle = jax.random.permutation(key_pool, pool_offset.shape[0])
        others = (hot_expert + pool_offset[shuffle[:remaining]]) % EXPERTS
        labels = jnp.concatenate([jnp.full((CAP,), hot_expert, jnp.int32), others.astype(jnp.int32)])
        return labels[jax.random.permutation(key_rows, TOK_DEV)]
    return jax.vmap(one_block)(block_keys, hot_blocks).reshape(TOKENS).astype(jnp.int32)


def shard_levels(rng, dims, cuts, smallest, high):
    gain = 1.0
    for dim, parts in cuts:
        draws = jax.random.uniform(jax.random.fold_in(jax.random.fold_in(rng, 6), dim), (parts,), jnp.float32, smallest / len(cuts), high / len(cuts))
        gain = gain * jnp.repeat(jnp.exp(draws), dims[dim] // parts).reshape((-1,) + (1,) * (len(dims) - 1 - dim))
    return gain


def gaussian(own_key, shape, width, bound, cuts=(), held_as=jnp.bfloat16):
    gain = shard_levels(own_key, shape, cuts, -0.22, 0.18) if cuts else 1.0
    result = jax.random.normal(own_key, shape, jnp.float32) * width * gain
    return jnp.minimum(jnp.maximum(result, -bound), bound).astype(held_as)


def setup_inputs(seed: int = 0) -> dict:
    key_of = jax.random.split(jax.random.key(seed), 7)
    return {
        "tokens": gaussian(key_of[0], (TOKENS, D), 1.0, 6.0, ((0, 256),)),
        "out_grad": gaussian(key_of[1], (TOKENS, D), 0.5, 3.0, ((0, 256),)),
        "gate_prob": jnp.clip(0.19921875 + 0.80078125 * jax.random.uniform(key_of[2], (TOKENS,), jnp.float32) ** shard_levels(key_of[2], (TOKENS,), ((0, 256),), -0.2, 0.2), 0.19921875, 1.0).astype(jnp.bfloat16),
        "expert_id": draw_expert_id(jax.random.fold_in(key_of[6], 71), 0),
        "up_weight": gaussian(key_of[4], (EXPERTS, D, FF), D ** -0.5, 0.1875, ((0, 16),)),
        "down_weight": gaussian(key_of[5], (EXPERTS, FF, D), FF ** -0.5, 0.125, ((0, 16),)),
    }


SQRT_HALF = 0.7071067811865476
INV_ROOT_TAU = 0.3989422804014327


def gelu_value(pre_act):
    return 0.5 * pre_act * (1.0 + jax.scipy.special.erf(pre_act * SQRT_HALF))


def gelu_slope(pre_act):
    normal_cdf = 0.5 * (1.0 + jax.scipy.special.erf(pre_act * SQRT_HALF))
    return normal_cdf + pre_act * jnp.exp(-0.5 * pre_act * pre_act) * INV_ROOT_TAU


def contract_rows(left, right):
    return lax.dot_general(left.astype(jnp.float32), right.astype(jnp.float32), (((0,), (0,)), ((), ())), preferred_element_type=jnp.float32)


def expert_rows(feat_rows, grad_rows, gate_rows, up_matrix, down_matrix):
    pre_act = jnp.dot(feat_rows, up_matrix, preferred_element_type=jnp.float32)
    hidden = gelu_value(pre_act).astype(jnp.bfloat16)
    expert_out = jnp.dot(hidden, down_matrix, preferred_element_type=jnp.float32)
    gate_grad = jnp.sum(grad_rows.astype(jnp.float32) * expert_out, axis=1).astype(jnp.bfloat16)
    scaled = (gate_rows.astype(jnp.float32)[:, None] * grad_rows.astype(jnp.float32)).astype(jnp.bfloat16)
    hidden_grad = jnp.dot(scaled, down_matrix.T, preferred_element_type=jnp.float32)
    pre_grad = (hidden_grad * gelu_slope(pre_act)).astype(jnp.bfloat16)
    feat_grad = jnp.dot(pre_grad, up_matrix.T, preferred_element_type=jnp.float32).astype(jnp.bfloat16)
    return feat_grad, gate_grad, hidden, scaled, pre_grad


def reference(tokens, out_grad, gate_prob, expert_id, up_weight, down_weight):
    group_rows = N_EXPERT * TOK_DEV
    slot_total = N_EXPERT * CAP
    feat_groups = tokens.reshape(N_DP, group_rows, D)
    grad_groups = out_grad.reshape(N_DP, group_rows, D)
    gate_groups = gate_prob.reshape(N_DP, group_rows)
    label_groups = expert_id.reshape(N_DP, group_rows)

    def per_group(running, inputs):
        up_total, down_total = running
        feat_group, grad_group, gate_group, label_group = inputs

        def per_expert(totals, expert):
            feat_acc, gate_acc = totals
            row_index = jnp.nonzero(label_group == expert, size=slot_total, fill_value=group_rows)[0].astype(jnp.int32)
            feat_rows = jnp.take(feat_group, row_index, axis=0, mode="fill", fill_value=0)
            grad_rows = jnp.take(grad_group, row_index, axis=0, mode="fill", fill_value=0)
            gate_rows = jnp.take(gate_group, row_index, axis=0, mode="fill", fill_value=0)
            feat_grad, gate_grad, hidden, scaled, pre_grad = expert_rows(feat_rows, grad_rows, gate_rows, up_weight[expert], down_weight[expert])
            up_part = lax.optimization_barrier(contract_rows(feat_rows, pre_grad).astype(jnp.bfloat16))
            down_part = lax.optimization_barrier(contract_rows(hidden, scaled).astype(jnp.bfloat16))
            feat_acc = feat_acc.at[row_index].set(feat_grad, mode="drop")
            gate_acc = gate_acc.at[row_index].set(gate_grad, mode="drop")
            return (feat_acc, gate_acc), (up_part, down_part)

        start_acc = (jnp.zeros((group_rows, D), jnp.bfloat16), jnp.zeros((group_rows,), jnp.bfloat16))
        (feat_acc, gate_acc), (up_parts, down_parts) = lax.scan(per_expert, start_acc, jnp.arange(EXPERTS, dtype=jnp.int32))
        return (up_total + up_parts.astype(jnp.float32), down_total + down_parts.astype(jnp.float32)), (feat_acc, gate_acc)

    start_sum = (jnp.zeros((EXPERTS, D, FF), jnp.float32), jnp.zeros((EXPERTS, FF, D), jnp.float32))
    (up_total, down_total), (feat_all, gate_all) = lax.scan(per_group, start_sum, (feat_groups, grad_groups, gate_groups, label_groups))
    divisor = 1.0 / N_DP
    return (feat_all.reshape(TOKENS, D), gate_all.reshape(TOKENS), up_total * divisor, down_total * divisor)
```

```python
import jax
import jax.numpy as jnp
from jax import lax
from jax.experimental import pallas as pl
from jax.experimental.pallas import tpu as pltpu
from jax.sharding import PartitionSpec as P

MESH = pl.DeviceIdType.MESH
SQRT_HALF = 0.7071067811865476
INV_ROOT_TAU = 0.3989422804014327
BF = jnp.bfloat16
F32 = jnp.float32
D = 1024
FF = 2048
TOK = 256
CAP = 32
NY = 4
NZ = 4
LANES = 128


def dot(a, b, ca, cb):
    return lax.dot_general(a, b, (((ca,), (cb,)), ((), ())), preferred_element_type=F32)


def iota(shape, axis):
    return lax.broadcasted_iota(jnp.int32, shape, axis)


def to_column(row):
    n = row.shape[1]
    eye = iota((n, n), 0) == iota((n, n), 1)
    return jnp.sum(jnp.where(eye, row, 0.0), axis=1, keepdims=True)


def kernel(
    tok_hbm, og_hbm, gate_ref, id_ref, upw_hbm, dnw_hbm,
    tg_ref, gg_ref, ug_ref, dg_ref,
    tok, og, upw, dnw, slots, recv, hidden, pregrad, fgs, back, ggs, ggback,
    s1u, s1d, ou, od, du, dd, r1u, r1d, rou, rod, rdu, rdd,
    zu, zd, zlu, zld, zru, zrd, fu, fd, pu, su, sd,
    in_sem, ds_sem, dr_sem, bs_sem, br_sem, gs_sem, gr_sem, ys_sem, yr_sem, zs_sem, zl_sem, zr_sem,
):
    dp = lax.axis_index("dp")
    ex = lax.axis_index("expert")
    y, zl = dp // NZ, dp % NZ
    zh, j = ex // 8, ex % 8

    def group_dp(h):
        return y * NZ + (NZ - 1 - zl) if h else dp

    def group_ex(h, other):
        return ((1 - zh) if h else zh) * 8 + other

    def dest(h, i):
        return (group_dp(h), group_ex(h, (j + i) % 8))

    def source(h, i):
        return (group_dp(h), group_ex(h, (j + 8 - i) % 8))

    plus = (((y + 1) % NY) * NZ + zl, ex)
    minus = (((y + NY - 1) % NY) * NZ + zl, ex)
    right = (dp + 1, ex)
    left = (dp - 1, ex)
    pairs = [(h, i) for h in (1, 0) for i in range(8) if (h, i) != (0, 0)]

    loads = [
        pltpu.make_async_copy(src, dst, in_sem.at[n])
        for n, (src, dst) in enumerate(
            ((tok_hbm, tok), (og_hbm, og), (upw_hbm, upw), (dnw_hbm, dnw))
        )
    ]
    for load in loads:
        load.start()

    barrier = pltpu.get_barrier_semaphore()
    for h, i in pairs:
        pl.semaphore_signal(barrier, inc=1, device_id=dest(h, i), device_id_type=MESH)
    for who in (plus, minus):
        pl.semaphore_signal(barrier, inc=1, device_id=who, device_id_type=MESH)

    @pl.when(zl < NZ - 1)
    def _():
        pl.semaphore_signal(barrier, inc=1, device_id=right, device_id_type=MESH)

    @pl.when(zl > 0)
    def _():
        pl.semaphore_signal(barrier, inc=1, device_id=left, device_id_type=MESH)

    ids = id_ref[...]
    ids_row = ids.astype(F32)
    ids_col = to_column(ids_row)
    same = ids_col == ids_row
    before = iota((TOK, TOK), 0) < iota((TOK, TOK), 1)
    after = iota((TOK, TOK), 1) < iota((TOK, TOK), 0)
    pos_row = jnp.sum(jnp.where(same & before, 1.0, 0.0), axis=0, keepdims=True)
    pos_col = jnp.sum(jnp.where(same & after, 1.0, 0.0), axis=1, keepdims=True)

    def slot_of(ident, place):
        mine = zh.astype(F32)
        half = jnp.where(ident >= 8.0, 1.0, 0.0)
        rank = ident - 8.0 * half - j.astype(F32)
        rank = jnp.where(rank < 0.0, rank + 8.0, rank)
        cross = jnp.abs(half - mine)
        return cross * 256.0 + rank * 32.0 + place

    slot_row = slot_of(ids_row, pos_row)
    slot_col = slot_of(ids_col, pos_col)
    gate_row = gate_ref[...].astype(F32)
    gate_col = to_column(gate_row)

    loads[0].wait()
    loads[1].wait()
    og[...] = (gate_col * og[...].astype(F32)).astype(BF)

    pl.semaphore_wait(barrier, 17 + (zl < NZ - 1).astype(jnp.int32) + (zl > 0).astype(jnp.int32))

    def dispatch(h, i):
        return pltpu.make_async_remote_copy(
            src_ref=slots.at[h, i], dst_ref=recv.at[h, i],
            send_sem=ds_sem.at[h, i], recv_sem=dr_sem.at[h, i],
            device_id=dest(h, i), device_id_type=MESH,
        )

    for h in (1, 0):
        place = (iota((TOK, TOK), 0) + TOK * h).astype(F32)
        pick = jnp.where(place == slot_row, 1.0, 0.0).astype(BF)
        slots[h, :, :CAP, :] = dot(pick, tok[...], 1, 0).astype(BF).reshape(8, CAP, D)
        slots[h, :, CAP:, :] = dot(pick, og[...], 1, 0).astype(BF).reshape(8, CAP, D)
        for i in range(8):
            if (h, i) != (0, 0):
                dispatch(h, i).start()
    recv[0, 0] = slots[0, 0]
    loads[2].wait()
    loads[3].wait()

    def rows_of(h, q):
        return pl.ds((h * 2 + q) * LANES, LANES)

    def forward(h, q):
        rows = rows_of(h, q)
        for i in range(4 * q, 4 * q + 4):
            if (h, i) != (0, 0):
                dispatch(h, i).wait_recv()

        def body(n, acc):
            cols = pl.ds(pl.multiple_of(n * 512, 512), 512)
            feat = recv[h, 4 * q : 4 * q + 4, :CAP, :].reshape(LANES, D)
            scaled = recv[h, 4 * q : 4 * q + 4, CAP:, :].reshape(LANES, D)
            pre = dot(feat, upw[:, cols], 1, 0)
            hgrad = dot(scaled, dnw[cols, :], 1, 1)
            cdf = 0.5 * (1.0 + lax.erf(pre * SQRT_HALF))
            hid = (pre * cdf).astype(BF)
            slope = cdf + pre * jnp.exp(-0.5 * pre * pre) * INV_ROOT_TAU
            hidden[rows, cols] = hid
            pregrad[rows, cols] = (hgrad * slope).astype(BF)
            return acc + jnp.sum(hid.astype(F32) * hgrad, axis=1, keepdims=True)

        total = lax.fori_loop(0, FF // 512, body, jnp.zeros((LANES, 1), F32))
        eye = iota((CAP, LANES), 0) == iota((CAP, LANES), 1)
        for i in range(4):
            part = total[i * CAP : (i + 1) * CAP, :]
            row = jnp.sum(jnp.where(eye, part, 0.0), axis=0, keepdims=True)
            ggs[h, 4 * q + i] = jnp.broadcast_to(row, (8, LANES))

    def give_back(h, i):
        return pltpu.make_async_remote_copy(
            src_ref=fgs.at[h, i], dst_ref=back.at[h, i],
            send_sem=bs_sem.at[h, i], recv_sem=br_sem.at[h, i],
            device_id=source(h, i), device_id_type=MESH,
        )

    def give_gate(h, i):
        return pltpu.make_async_remote_copy(
            src_ref=ggs.at[h, i], dst_ref=ggback.at[h, i],
            send_sem=gs_sem.at[h, i], recv_sem=gr_sem.at[h, i],
            device_id=source(h, i), device_id_type=MESH,
        )

    def feature_grad(h, q):
        rows = rows_of(h, q)

        @pl.loop(0, D // 512)
        def _(n):
            cols = pl.ds(pl.multiple_of(n * 512, 512), 512)
            fg = dot(pregrad[rows, :], upw[cols, :], 1, 1).astype(BF)
            fgs[h, 4 * q : 4 * q + 4, :, cols] = fg.reshape(4, CAP, 512)

        for i in range(4 * q, 4 * q + 4):
            if (h, i) == (0, 0):
                back[0, 0] = fgs[0, 0]
                ggback[0, 0] = ggs[0, 0]
            else:
                give_back(h, i).start()
                give_gate(h, i).start()

    forward(0, 0)
    forward(0, 1)
    feature_grad(0, 0)
    feature_grad(0, 1)
    forward(1, 0)
    forward(1, 1)

    def up_pair(chunk, m, emit):
        @pl.loop(0, FF // 512)
        def _(n):
            cols = pl.ds(pl.multiple_of(n * 512, 512), 512)
            feats = pl.ds(pl.multiple_of(chunk * 256 + m * LANES, LANES), LANES)
            lhs = recv[:, :, :CAP, feats].reshape(512, LANES)
            emit(cols, dot(lhs, pregrad[:, cols], 0, 0))

    def down_block(chunk, k, emit):
        @pl.loop(0, D // 512)
        def _(n):
            cols = pl.ds(pl.multiple_of(n * 512, 512), 512)
            feats = pl.ds(pl.multiple_of(chunk * 512 + k * LANES, LANES), LANES)
            rhs = recv[:, :, CAP:, cols].reshape(512, 512)
            emit(cols, dot(hidden[:, feats], rhs, 0, 0))

    yrefs = (
        (s1u, r1u, plus), (s1d, r1d, minus), (ou, rou, minus),
        (od, rod, plus), (du, rdu, plus), (dd, rdd, minus),
    )

    def ysend(which, k):
        src, dst, who = yrefs[which]
        return pltpu.make_async_remote_copy(
            src_ref=src.at[k], dst_ref=dst.at[k],
            send_sem=ys_sem.at[which, k], recv_sem=yr_sem.at[which, k],
            device_id=who, device_id_type=MESH,
        )

    S1U, S1D, OU, OD, DU, DD = range(6)
    far, nxt, prv = (y + 2) % NY, (y + 1) % NY, (y + NY - 1) % NY

    def order(m, s):
        return 2 * m + (s + m) % 2

    def store_pair(ref, m):
        def emit(cols, v):
            ref[2 * m, :, cols] = v[:64].astype(BF)
            ref[2 * m + 1, :, cols] = v[64:].astype(BF)

        return emit

    def add_pair(ref, other, m):
        def emit(cols, v):
            ref[2 * m, :, cols] = (v[:64] + other[2 * m, :, cols].astype(F32)).astype(BF)
            ref[2 * m + 1, :, cols] = (v[64:] + other[2 * m + 1, :, cols].astype(F32)).astype(BF)

        return emit

    def store_block(ref, k):
        def emit(cols, v):
            ref[k, :, cols] = v.astype(BF)

        return emit

    def add_block(ref, other, k):
        def emit(cols, v):
            ref[k, :, cols] = (v + other[k, :, cols].astype(F32)).astype(BF)

        return emit

    @pl.loop(0, 2)
    def _(m):
        up_pair(far, m, store_pair(s1u, m))
        for s in range(2):
            k = order(m, s)
            ysend(S1U, k).start()
            down_block(far, k, store_block(s1d, k))
            ysend(S1D, k).start()

    feature_grad(1, 0)
    feature_grad(1, 1)

    @pl.loop(0, 2)
    def _(m):
        up_pair(prv, m, store_pair(ou, m))
        for s in range(2):
            ysend(S1U, order(m, s)).wait_recv()
        up_pair(nxt, m, add_pair(du, r1u, m))
        for s in range(2):
            k = order(m, s)
            ysend(OU, k).start()
            down_block(nxt, k, store_block(od, k))
            ysend(OD, k).start()
            ysend(DU, k).start()
            ysend(S1D, k).wait_recv()
            down_block(prv, k, add_block(dd, r1d, k))
            ysend(DD, k).start()

    for h, i in pairs:
        give_back(h, i).wait_recv()
        give_gate(h, i).wait_recv()
    spread = jnp.where(iota((TOK, 512), 1).astype(F32) == slot_col, 1.0, 0.0).astype(BF)

    @pl.loop(0, D // 512)
    def _(n):
        cols = pl.ds(pl.multiple_of(n * 512, 512), 512)
        rows = back[:, :, :, cols].reshape(512, 512)
        tg_ref[:, cols] = dot(spread, rows, 1, 0).astype(BF)

    lane = iota((TOK, LANES), 1).astype(F32)
    gate_sum = jnp.zeros((TOK, LANES), F32)
    for h in range(2):
        for i in range(8):
            base = float(h * 256 + i * CAP)
            hit = (lane < float(CAP)) & (lane + base == slot_col)
            gate_sum += jnp.where(hit, ggback[h, i, 0:1, :], 0.0)
    gate_total = jnp.sum(gate_sum, axis=1, keepdims=True) / gate_col
    eye = iota((TOK, TOK), 0) == iota((TOK, TOK), 1)
    gg_ref[...] = jnp.sum(jnp.where(eye, gate_total, 0.0), axis=0, keepdims=True).astype(BF)

    zrefs = ((zu, zlu, zru), (zd, zld, zrd))

    def zright(t, k):
        src, dst, _ = zrefs[t]
        return pltpu.make_async_remote_copy(
            src_ref=src.at[k], dst_ref=dst.at[k],
            send_sem=zs_sem.at[t, k], recv_sem=zl_sem.at[t, k],
            device_id=right, device_id_type=MESH,
        )

    def zleft(t, k):
        src, _, dst = zrefs[t]
        return pltpu.make_async_remote_copy(
            src_ref=src.at[k], dst_ref=dst.at[k],
            send_sem=zs_sem.at[t, k], recv_sem=zr_sem.at[t, k],
            device_id=left, device_id_type=MESH,
        )

    def line(t, k, total, final):
        out, from_left, from_right = zrefs[t]

        @pl.when(zl == k)
        def _():
            final[...] = total[...]

        @pl.when((zl < k) & (zl == 0))
        def _():
            out[k] = total[...].astype(BF)

        @pl.when((zl < k) & (zl > 0))
        def _():
            zright(t, k).wait_recv()
            out[k] = (total[...] + from_left[k].astype(F32)).astype(BF)

        @pl.when(zl < k)
        def _():
            zright(t, k).start()

        @pl.when((zl > k) & (zl == NZ - 1))
        def _():
            out[k] = total[...].astype(BF)

        @pl.when((zl > k) & (zl < NZ - 1))
        def _():
            zleft(t, k).wait_recv()
            out[k] = (total[...] + from_right[k].astype(F32)).astype(BF)

        @pl.when(zl > k)
        def _():
            zleft(t, k).start()

    @pl.loop(0, 2)
    def _(m):
        def emit_pu(cols, v):
            pu[0, :, cols] = v[:64]
            pu[1, :, cols] = v[64:]

        up_pair(y, m, emit_pu)
        for s in range(2):
            k = order(m, s)

            def emit_sd(cols, v):
                sd[:, cols] = v

            down_block(y, k, emit_sd)
            ysend(DU, k).wait_recv()
            ysend(OU, k).wait_recv()
            su[...] = pu[(s + m) % 2] + rdu[k].astype(F32) + rou[k].astype(F32)
            line(0, k, su, fu)
            ysend(OD, k).wait_recv()
            ysend(DD, k).wait_recv()
            sd[...] = sd[...] + rod[k].astype(F32) + rdd[k].astype(F32)
            line(1, k, sd, fd)

    for t, final in ((0, fu), (1, fd)):
        _, from_left, from_right = zrefs[t]

        @pl.when(zl > 0)
        def _():
            zright(t, zl).wait_recv()
            final[...] = final[...] + from_left[zl].astype(F32)

        @pl.when(zl < NZ - 1)
        def _():
            zleft(t, zl).wait_recv()
            final[...] = final[...] + from_right[zl].astype(F32)

    scale = 1.0 / (NY * NZ)
    ug_ref[...] = fu[...] * scale
    dg_ref[...] = fd[...] * scale

    for h, i in pairs:
        dispatch(h, i).wait_send()
        give_back(h, i).wait_send()
        give_gate(h, i).wait_send()

    @pl.loop(0, 4)
    def _(k):
        for which in range(6):
            ysend(which, k).wait_send()

        @pl.when(zl != k)
        def _():
            zright(0, k).wait_send()
            zright(1, k).wait_send()


def per_device(tokens, out_grad, gate_prob, expert_id, up_weight, down_weight):
    any_spec = pl.BlockSpec(memory_space=pl.ANY)
    vmem = pl.BlockSpec(memory_space=pltpu.VMEM)
    up_blocks = pltpu.VMEM((4, 64, FF), BF)
    down_blocks = pltpu.VMEM((4, 128, D), BF)
    dma = pltpu.SemaphoreType.DMA
    tg, gg, ug, dg = pl.pallas_call(
        kernel,
        out_shape=(
            jax.ShapeDtypeStruct((TOK, D), BF),
            jax.ShapeDtypeStruct((1, TOK), BF),
            jax.ShapeDtypeStruct((64, FF), F32),
            jax.ShapeDtypeStruct((128, D), F32),
        ),
        in_specs=[any_spec, any_spec, vmem, vmem, any_spec, any_spec],
        out_specs=(vmem, vmem, vmem, vmem),
        scratch_shapes=[
            pltpu.VMEM((TOK, D), BF),
            pltpu.VMEM((TOK, D), BF),
            pltpu.VMEM((D, FF), BF),
            pltpu.VMEM((FF, D), BF),
            pltpu.VMEM((2, 8, 2 * CAP, D), BF),
            pltpu.VMEM((2, 8, 2 * CAP, D), BF),
            pltpu.VMEM((512, FF), BF),
            pltpu.VMEM((512, FF), BF),
            pltpu.VMEM((2, 8, CAP, D), BF),
            pltpu.VMEM((2, 8, CAP, D), BF),
            pltpu.VMEM((2, 8, 8, LANES), F32),
            pltpu.VMEM((2, 8, 8, LANES), F32),
            up_blocks, down_blocks, up_blocks, down_blocks, up_blocks, down_blocks,
            up_blocks, down_blocks, up_blocks, down_blocks, up_blocks, down_blocks,
            up_blocks, down_blocks, up_blocks, down_blocks, up_blocks, down_blocks,
            pltpu.VMEM((64, FF), F32),
            pltpu.VMEM((128, D), F32),
            pltpu.VMEM((2, 64, FF), F32),
            pltpu.VMEM((64, FF), F32),
            pltpu.VMEM((128, D), F32),
            dma((4,)),
            dma((2, 8)), dma((2, 8)), dma((2, 8)), dma((2, 8)), dma((2, 8)), dma((2, 8)),
            dma((6, 4)), dma((6, 4)), dma((2, 4)), dma((2, 4)), dma((2, 4)),
        ],
        compiler_params=pltpu.CompilerParams(
            collective_id=0, has_side_effects=True, vmem_limit_bytes=60 * 1024 * 1024
        ),
    )(
        tokens,
        out_grad,
        gate_prob.reshape(1, TOK),
        expert_id.reshape(1, TOK),
        up_weight[0],
        down_weight[0],
    )
    return tg, gg.reshape(TOK), ug[None], dg[None]


def solution(mesh):
    return jax.shard_map(
        per_device,
        mesh=mesh,
        in_specs=(
            P(("dp", "expert"), None),
            P(("dp", "expert"), None),
            P(("dp", "expert")),
            P(("dp", "expert")),
            P("expert", None, None),
            P("expert", None, None),
        ),
        out_specs=(
            P(("dp", "expert"), None),
            P(("dp", "expert")),
            P("expert", "dp", None),
            P("expert", "dp", None),
        ),
        check_vma=False,
    )
```

```python
import jax
import jax.numpy as jnp
from jax import lax
from jax.experimental import pallas as pl
from jax.experimental.pallas import tpu as pltpu
from jax.sharding import PartitionSpec as P

MESH = pl.DeviceIdType.MESH
SQRT_HALF = 0.7071067811865476
INV_ROOT_TAU = 0.3989422804014327
BF = jnp.bfloat16
F32 = jnp.float32
D = 1024
FF = 2048
TOK = 256
CAP = 32
NY = 4
NZ = 4
LANES = 128


def dot(a, b, ca, cb):
    return lax.dot_general(a, b, (((ca,), (cb,)), ((), ())), preferred_element_type=F32)


def iota(shape, axis):
    return lax.broadcasted_iota(jnp.int32, shape, axis)


def to_column(row):
    n = row.shape[1]
    eye = iota((n, n), 0) == iota((n, n), 1)
    return jnp.sum(jnp.where(eye, row, 0.0), axis=1, keepdims=True)


def kernel(
    tok_hbm, og_hbm, gate_ref, id_ref, upw_hbm, dnw_hbm,
    tg_ref, gg_ref, ug_ref, dg_ref,
    tok, og, upw, dnw, slots, rows, hidden, pregrad, fgp, fgr, fgs, back,
    gown, gp, gr, ggs, ggback,
    su_out, sd_out, su_in, sd_in, zu, zd, zlu, zld, zru, zrd, fu, fd, xu, pu, su, sd,
    in_sem, ds_sem, dr_sem, as_sem, ar_sem, fs_sem, fr_sem, hs_sem, hr_sem,
    bs_sem, br_sem, gs_sem, gr_sem, ys_sem, yr_sem, zs_sem, zl_sem, zr_sem, xs_sem, xr_sem,
):
    dp = lax.axis_index("dp")
    ex = lax.axis_index("expert")
    y, zl = dp // NZ, dp % NZ
    zh, j = ex // 8, ex % 8
    core = ex % 2
    near = y + 1 - 2 * (y % 2)
    flip = NY - 1 - y
    yr = near + core * (flip - near)
    yf = flip + core * (near - flip)
    yd = (y + 2) % NY

    def group_dp(h):
        return y * NZ + (NZ - 1 - zl) if h else dp

    def group_ex(h, other):
        return ((1 - zh) if h else zh) * 8 + other

    def dest(h, i):
        return (group_dp(h), group_ex(h, (j + i) % 8))

    def source(h, i):
        return (group_dp(h), group_ex(h, (j + 8 - i) % 8))

    mate = (yr * NZ + zl, ex)
    twin = (yf * NZ + zl, ex)
    right = (dp + 1, ex)
    left = (dp - 1, ex)
    pairs = [(h, i) for h in (1, 0) for i in range(8) if (h, i) != (0, 0)]

    sources = [
        (tok_hbm, tok),
        (og_hbm, og),
        (upw_hbm.at[:, pl.ds(pl.multiple_of(y * 512, 512), 512)], upw.at[:, 0:512]),
        (upw_hbm.at[:, pl.ds(pl.multiple_of(yf * 512, 512), 512)], upw.at[:, 512:1024]),
        (dnw_hbm.at[pl.ds(pl.multiple_of(y * 512, 512), 512), :], dnw.at[0:512, :]),
        (dnw_hbm.at[pl.ds(pl.multiple_of(yf * 512, 512), 512), :], dnw.at[512:1024, :]),
    ]
    loads = [
        pltpu.make_async_copy(src, dst, in_sem.at[n]) for n, (src, dst) in enumerate(sources)
    ]
    for load in loads:
        load.start()

    barrier = pltpu.get_barrier_semaphore()
    for h, i in pairs:
        pl.semaphore_signal(barrier, inc=1, device_id=dest(h, i), device_id_type=MESH)
    for who in (mate, twin):
        pl.semaphore_signal(barrier, inc=1, device_id=who, device_id_type=MESH)

    @pl.when(zl < NZ - 1)
    def _():
        pl.semaphore_signal(barrier, inc=1, device_id=right, device_id_type=MESH)

    @pl.when(zl > 0)
    def _():
        pl.semaphore_signal(barrier, inc=1, device_id=left, device_id_type=MESH)

    ids = id_ref[...]
    ids_row = ids.astype(F32)
    ids_col = to_column(ids_row)
    same = ids_col == ids_row
    before = iota((TOK, TOK), 0) < iota((TOK, TOK), 1)
    after = iota((TOK, TOK), 1) < iota((TOK, TOK), 0)
    pos_row = jnp.sum(jnp.where(same & before, 1.0, 0.0), axis=0, keepdims=True)
    pos_col = jnp.sum(jnp.where(same & after, 1.0, 0.0), axis=1, keepdims=True)

    def slot_of(ident, place):
        mine = zh.astype(F32)
        half = jnp.where(ident >= 8.0, 1.0, 0.0)
        rank = ident - 8.0 * half - j.astype(F32)
        rank = jnp.where(rank < 0.0, rank + 8.0, rank)
        cross = jnp.abs(half - mine)
        return cross * 256.0 + rank * 32.0 + place

    slot_row = slot_of(ids_row, pos_row)
    slot_col = slot_of(ids_col, pos_col)
    gate_row = gate_ref[...].astype(F32)
    gate_col = to_column(gate_row)

    loads[0].wait()
    loads[1].wait()
    og[...] = (gate_col * og[...].astype(F32)).astype(BF)

    pl.semaphore_wait(barrier, 17 + (zl < NZ - 1).astype(jnp.int32) + (zl > 0).astype(jnp.int32))

    def dispatch(h, i):
        return pltpu.make_async_remote_copy(
            src_ref=slots.at[h, i], dst_ref=rows.at[0, h, i],
            send_sem=ds_sem.at[h, i], recv_sem=dr_sem.at[h, i],
            device_id=dest(h, i), device_id_type=MESH,
        )

    def relay(h, i):
        src = slots.at[0, 0] if (h, i) == (0, 0) else rows.at[0, h, i]
        return pltpu.make_async_remote_copy(
            src_ref=src, dst_ref=rows.at[1, h, i],
            send_sem=as_sem.at[h, i], recv_sem=ar_sem.at[h, i],
            device_id=mate, device_id_type=MESH,
        )

    for h in (1, 0):
        place = (iota((TOK, TOK), 0) + TOK * h).astype(F32)
        pick = jnp.where(place == slot_row, 1.0, 0.0).astype(BF)
        slots[h, :, :CAP, :] = dot(pick, tok[...], 1, 0).astype(BF).reshape(8, CAP, D)
        slots[h, :, CAP:, :] = dot(pick, og[...], 1, 0).astype(BF).reshape(8, CAP, D)
        for i in range(8):
            if (h, i) != (0, 0):
                dispatch(h, i).start()
    relay(0, 0).start()
    rows[0, 0, 0] = slots[0, 0]
    for load in loads[2:]:
        load.wait()

    def rows_of(who, h, q):
        return pl.ds(who * 512 + (h * 2 + q) * LANES, LANES)

    def forward(who, h, q):
        here = rows_of(who, h, q)

        def body(n, acc):
            cols = pl.ds(pl.multiple_of(n * 512, 512), 512)
            feat = rows[who, h, 4 * q : 4 * q + 4, :CAP, :].reshape(LANES, D)
            scaled = rows[who, h, 4 * q : 4 * q + 4, CAP:, :].reshape(LANES, D)
            pre = dot(feat, upw[:, cols], 1, 0)
            hgrad = dot(scaled, dnw[cols, :], 1, 1)
            cdf = 0.5 * (1.0 + lax.erf(pre * SQRT_HALF))
            hid = (pre * cdf).astype(BF)
            slope = cdf + pre * jnp.exp(-0.5 * pre * pre) * INV_ROOT_TAU
            hidden[here, cols] = hid
            pregrad[here, cols] = (hgrad * slope).astype(BF)
            return acc + jnp.sum(hid.astype(F32) * hgrad, axis=1, keepdims=True)

        total = lax.fori_loop(0, 2, body, jnp.zeros((LANES, 1), F32))
        eye = iota((CAP, LANES), 0) == iota((CAP, LANES), 1)
        out = gp if who else gown
        for i in range(4):
            part = total[i * CAP : (i + 1) * CAP, :]
            row = jnp.sum(jnp.where(eye, part, 0.0), axis=0, keepdims=True)
            out[h, 4 * q + i] = jnp.broadcast_to(row, (8, LANES))

    def share_fg(h, q):
        return pltpu.make_async_remote_copy(
            src_ref=fgp.at[h, 4 * q : 4 * q + 4], dst_ref=fgr.at[h, 4 * q : 4 * q + 4],
            send_sem=fs_sem.at[h, q], recv_sem=fr_sem.at[h, q],
            device_id=mate, device_id_type=MESH,
        )

    def share_gate(h, q):
        return pltpu.make_async_remote_copy(
            src_ref=gp.at[h, 4 * q : 4 * q + 4], dst_ref=gr.at[h, 4 * q : 4 * q + 4],
            send_sem=hs_sem.at[h, q], recv_sem=hr_sem.at[h, q],
            device_id=mate, device_id_type=MESH,
        )

    def give_back(h, i):
        return pltpu.make_async_remote_copy(
            src_ref=fgs.at[h, i], dst_ref=back.at[h, i],
            send_sem=bs_sem.at[h, i], recv_sem=br_sem.at[h, i],
            device_id=source(h, i), device_id_type=MESH,
        )

    def give_gate(h, i):
        return pltpu.make_async_remote_copy(
            src_ref=ggs.at[h, i], dst_ref=ggback.at[h, i],
            send_sem=gs_sem.at[h, i], recv_sem=gr_sem.at[h, i],
            device_id=source(h, i), device_id_type=MESH,
        )

    def feature_part(who, h, q, emit):
        here = rows_of(who, h, q)

        @pl.loop(0, D // 512)
        def _(n):
            cols = pl.ds(pl.multiple_of(n * 512, 512), 512)
            emit(cols, dot(pregrad[here, :], upw[cols, :], 1, 1).reshape(4, CAP, 512))

    def mate_part(h, q):
        def emit(cols, v):
            fgp[h, 4 * q : 4 * q + 4, :, cols] = v.astype(BF)

        feature_part(1, h, q, emit)
        share_fg(h, q).start()
        share_gate(h, q).start()

    def finish(h, q):
        some = slice(4 * q, 4 * q + 4)
        share_fg(h, q).wait_recv()
        share_gate(h, q).wait_recv()

        def emit(cols, v):
            fgs[h, some, :, cols] = (v + fgr[h, some, :, cols].astype(F32)).astype(BF)

        feature_part(0, h, q, emit)
        ggs[h, some] = gown[h, some] + gr[h, some]
        for i in range(4 * q, 4 * q + 4):
            if (h, i) == (0, 0):
                back[0, 0] = fgs[0, 0]
                ggback[0, 0] = ggs[0, 0]
            else:
                give_back(h, i).start()
                give_gate(h, i).start()

    last = None
    for h, q in ((0, 0), (0, 1), (1, 0), (1, 1)):
        for i in range(4 * q, 4 * q + 4):
            if (h, i) != (0, 0):
                dispatch(h, i).wait_recv()
                relay(h, i).start()
        forward(0, h, q)
        for i in range(4 * q, 4 * q + 4):
            relay(h, i).wait_recv()
        forward(1, h, q)
        mate_part(h, q)
        if last is not None:
            finish(*last)
        last = (h, q)

    def up_pair(first, second, m, emit):
        @pl.loop(0, 4)
        def _(t):
            c, n = t // 2, t % 2
            chunk = first + c * (second - first)
            cols = pl.ds(pl.multiple_of(n * 512, 512), 512)
            feats = pl.ds(pl.multiple_of(chunk * 256 + m * LANES, LANES), LANES)
            lhs = rows[:, :, :, :CAP, feats].reshape(1024, LANES)
            emit(c, n, dot(lhs, pregrad[:, cols], 0, 0))

    def down_block(half, k, emit):
        @pl.loop(0, D // 512)
        def _(n):
            cols = pl.ds(pl.multiple_of(n * 512, 512), 512)
            feats = pl.ds(pl.multiple_of(half * 512 + k * LANES, LANES), LANES)
            rhs = rows[:, :, :, CAP:, cols].reshape(1024, 512)
            emit(cols, dot(hidden[:, feats], rhs, 0, 0))

    def ysend(t, k):
        src, dst = ((su_out, su_in), (sd_out, sd_in))[t]
        return pltpu.make_async_remote_copy(
            src_ref=src.at[k], dst_ref=dst.at[k],
            send_sem=ys_sem.at[t, k], recv_sem=yr_sem.at[t, k],
            device_id=twin, device_id_type=MESH,
        )

    def order(m, s):
        return 2 * m + (s + m) % 2

    @pl.loop(0, 2)
    def _(m):
        def emit(c, n, v):
            cols = pl.ds(pl.multiple_of((1 - n) * 512, 512), 512)
            su_out[2 * m, c, :, cols] = v[:64].astype(BF)
            su_out[2 * m + 1, c, :, cols] = v[64:].astype(BF)

        up_pair(yf, yd, m, emit)
        for s in range(2):
            ysend(0, order(m, s)).start()

    @pl.loop(0, 2)
    def _(m):
        for s in range(2):
            k = order(m, s)

            def emit(cols, v):
                sd_out[k, :, cols] = v.astype(BF)

            down_block(1, k, emit)
            ysend(1, k).start()

    finish(*last)

    zrefs = ((zu, zlu, zru), (zd, zld, zrd))

    def zright(t, k):
        src, dst, _ = zrefs[t]
        return pltpu.make_async_remote_copy(
            src_ref=src.at[k], dst_ref=dst.at[k],
            send_sem=zs_sem.at[t, k], recv_sem=zl_sem.at[t, k],
            device_id=right, device_id_type=MESH,
        )

    def zleft(t, k):
        src, _, dst = zrefs[t]
        return pltpu.make_async_remote_copy(
            src_ref=src.at[k], dst_ref=dst.at[k],
            send_sem=zs_sem.at[t, k], recv_sem=zr_sem.at[t, k],
            device_id=left, device_id_type=MESH,
        )

    def line(t, k, total, final):
        out, from_left, from_right = zrefs[t]

        @pl.when(zl == k)
        def _():
            final[...] = total[...]

        @pl.when((zl < k) & (zl == 0))
        def _():
            out[k] = total[...].astype(BF)

        @pl.when((zl < k) & (zl > 0))
        def _():
            zright(t, k).wait_recv()
            out[k] = (total[...] + from_left[k].astype(F32)).astype(BF)

        @pl.when(zl < k)
        def _():
            zright(t, k).start()

        @pl.when((zl > k) & (zl == NZ - 1))
        def _():
            out[k] = total[...].astype(BF)

        @pl.when((zl > k) & (zl < NZ - 1))
        def _():
            zleft(t, k).wait_recv()
            out[k] = (total[...] + from_right[k].astype(F32)).astype(BF)

        @pl.when(zl > k)
        def _():
            zleft(t, k).start()

    @pl.loop(0, 2)
    def _(m):
        def emit_pu(c, n, v):
            cols = pl.ds(pl.multiple_of(n * 512, 512), 512)
            pu[0, c, :, cols] = v[:64]
            pu[1, c, :, cols] = v[64:]

        up_pair(y, yr, m, emit_pu)
        for s in range(2):
            k = order(m, s)
            ysend(0, k).wait_recv()
            su[...] = pu[(s + m) % 2] + su_in[k].astype(F32)
            line(0, k, su, fu)

    def down_line(m):
        for s in range(2):
            k = 2 * m + (s + m) % 2

            def emit_sd(cols, v):
                sd[:, cols] = v

            down_block(0, k, emit_sd)
            ysend(1, k).wait_recv()
            sd[...] = sd[...] + sd_in[k].astype(F32)
            line(1, k, sd, fd)

    def settle(t, final):
        _, from_left, from_right = zrefs[t]

        @pl.when(zl > 0)
        def _():
            zright(t, zl).wait_recv()
            final[...] = final[...] + from_left[zl].astype(F32)

        @pl.when(zl < NZ - 1)
        def _():
            zleft(t, zl).wait_recv()
            final[...] = final[...] + from_right[zl].astype(F32)

    down_line(0)
    settle(0, fu)
    swap = pltpu.make_async_remote_copy(
        src_ref=fu.at[1], dst_ref=xu,
        send_sem=xs_sem.at[0], recv_sem=xr_sem.at[0],
        device_id=mate, device_id_type=MESH,
    )
    swap.start()
    down_line(1)

    for h, i in pairs:
        give_back(h, i).wait_recv()
        give_gate(h, i).wait_recv()
    spread = jnp.where(iota((TOK, 512), 1).astype(F32) == slot_col, 1.0, 0.0).astype(BF)

    @pl.loop(0, D // 512)
    def _(n):
        cols = pl.ds(pl.multiple_of(n * 512, 512), 512)
        tg_ref[:, cols] = dot(spread, back[:, :, :, cols].reshape(512, 512), 1, 0).astype(BF)

    lane = iota((TOK, LANES), 1).astype(F32)
    gate_sum = jnp.zeros((TOK, LANES), F32)
    for h in range(2):
        for i in range(8):
            base = float(h * 256 + i * CAP)
            hit = (lane < float(CAP)) & (lane + base == slot_col)
            gate_sum += jnp.where(hit, ggback[h, i, 0:1, :], 0.0)
    gate_total = jnp.sum(gate_sum, axis=1, keepdims=True) / gate_col
    eye = iota((TOK, TOK), 0) == iota((TOK, TOK), 1)
    gg_ref[...] = jnp.sum(jnp.where(eye, gate_total, 0.0), axis=0, keepdims=True).astype(BF)

    scale = 1.0 / (NY * NZ)

    def ff_chunk(c):
        return pl.ds(pl.multiple_of(c * 512, 512), 512)

    swap.wait_recv()
    ug_ref[:, ff_chunk(y)] = fu[0, :, 0:512] * scale
    ug_ref[:, ff_chunk(yf)] = fu[0, :, 512:1024] * scale
    ug_ref[:, ff_chunk(yr)] = xu[:, 0:512] * scale
    ug_ref[:, ff_chunk(yd)] = xu[:, 512:1024] * scale
    settle(1, fd)
    dg_ref[...] = fd[...] * scale

    swap.wait_send()
    relay(0, 0).wait_send()
    for h, i in pairs:
        dispatch(h, i).wait_send()
        relay(h, i).wait_send()
        give_back(h, i).wait_send()
        give_gate(h, i).wait_send()
    for h in range(2):
        for q in range(2):
            share_fg(h, q).wait_send()
            share_gate(h, q).wait_send()

    @pl.loop(0, 4)
    def _(k):
        ysend(0, k).wait_send()
        ysend(1, k).wait_send()

        @pl.when(zl != k)
        def _():
            zright(0, k).wait_send()
            zright(1, k).wait_send()


def per_device(tokens, out_grad, gate_prob, expert_id, up_weight, down_weight):
    any_spec = pl.BlockSpec(memory_space=pl.ANY)
    vmem = pl.BlockSpec(memory_space=pltpu.VMEM)
    up_blocks = pltpu.VMEM((4, 2, 64, 1024), BF)
    down_blocks = pltpu.VMEM((4, 128, D), BF)
    grads = pltpu.VMEM((2, 8, CAP, D), BF)
    gates = pltpu.VMEM((2, 8, 8, LANES), F32)
    dma = pltpu.SemaphoreType.DMA
    tg, gg, ug, dg = pl.pallas_call(
        kernel,
        out_shape=(
            jax.ShapeDtypeStruct((TOK, D), BF),
            jax.ShapeDtypeStruct((1, TOK), BF),
            jax.ShapeDtypeStruct((64, FF), F32),
            jax.ShapeDtypeStruct((128, D), F32),
        ),
        in_specs=[any_spec, any_spec, vmem, vmem, any_spec, any_spec],
        out_specs=(vmem, vmem, vmem, vmem),
        scratch_shapes=[
            pltpu.VMEM((TOK, D), BF),
            pltpu.VMEM((TOK, D), BF),
            pltpu.VMEM((D, 1024), BF),
            pltpu.VMEM((1024, D), BF),
            pltpu.VMEM((2, 8, 2 * CAP, D), BF),
            pltpu.VMEM((2, 2, 8, 2 * CAP, D), BF),
            pltpu.VMEM((1024, 1024), BF),
            pltpu.VMEM((1024, 1024), BF),
            grads, grads, grads, grads,
            gates, gates, gates, gates, gates,
            up_blocks, down_blocks, up_blocks, down_blocks, up_blocks, down_blocks,
            up_blocks, down_blocks, up_blocks, down_blocks,
            pltpu.VMEM((2, 64, 1024), F32),
            pltpu.VMEM((128, D), F32),
            pltpu.VMEM((64, 1024), F32),
            pltpu.VMEM((2, 2, 64, 1024), F32),
            pltpu.VMEM((2, 64, 1024), F32),
            pltpu.VMEM((128, D), F32),
            dma((6,)),
            dma((2, 8)), dma((2, 8)), dma((2, 8)), dma((2, 8)),
            dma((2, 2)), dma((2, 2)), dma((2, 2)), dma((2, 2)),
            dma((2, 8)), dma((2, 8)), dma((2, 8)), dma((2, 8)),
            dma((2, 4)), dma((2, 4)), dma((2, 4)), dma((2, 4)), dma((2, 4)), dma((1,)), dma((1,)),
        ],
        compiler_params=pltpu.CompilerParams(
            collective_id=0, has_side_effects=True, vmem_limit_bytes=60 * 1024 * 1024
        ),
    )(
        tokens,
        out_grad,
        gate_prob.reshape(1, TOK),
        expert_id.reshape(1, TOK),
        up_weight[0],
        down_weight[0],
    )
    return tg, gg.reshape(TOK), ug[None], dg[None]


def solution(mesh):
    return jax.shard_map(
        per_device,
        mesh=mesh,
        in_specs=(
            P(("dp", "expert"), None),
            P(("dp", "expert"), None),
            P(("dp", "expert")),
            P(("dp", "expert")),
            P("expert", None, None),
            P("expert", None, None),
        ),
        out_specs=(
            P(("dp", "expert"), None),
            P(("dp", "expert")),
            P("expert", "dp", None),
            P("expert", "dp", None),
        ),
        check_vma=False,
    )
```

```python
import jax
import jax.numpy as jnp
from jax import lax
from jax.experimental import pallas as pl
from jax.experimental.pallas import tpu as pltpu
from jax.sharding import PartitionSpec as P

MESH = pl.DeviceIdType.MESH
SQRT_HALF = 0.7071067811865476
INV_ROOT_TAU = 0.3989422804014327
BF = jnp.bfloat16
F32 = jnp.float32
D = 1024
FF = 2048
TOK = 256
CAP = 32
NY = 4
NZ = 4
LANES = 128


def dot(a, b, ca, cb):
    return lax.dot_general(a, b, (((ca,), (cb,)), ((), ())), preferred_element_type=F32)


def iota(shape, axis):
    return lax.broadcasted_iota(jnp.int32, shape, axis)


def to_column(row):
    n = row.shape[1]
    eye = iota((n, n), 0) == iota((n, n), 1)
    return jnp.sum(jnp.where(eye, row, 0.0), axis=1, keepdims=True)


def kernel(
    tok_hbm, og_hbm, gate_ref, id_ref, upw_hbm, dnw_hbm,
    tg_ref, gg_ref, ug_ref, dg_ref,
    tok, og, upw, dnw, slots, rows, hidden, pregrad, fgp, fgr, fgs, back,
    gown, gp, gr, ggs, ggback,
    su_out, sd_out, su_in, sd_in, zu, zd, zlu, zld, zru, zrd, fu, fd, xu, pu, pd,
    in_sem, ds_sem, dr_sem, as_sem, ar_sem, fs_sem, fr_sem, hs_sem, hr_sem,
    bs_sem, br_sem, gs_sem, gr_sem, ys_sem, yr_sem, zs_sem, zl_sem, zr_sem, xs_sem, xr_sem,
):
    dp = lax.axis_index("dp")
    ex = lax.axis_index("expert")
    y, zl = dp // NZ, dp % NZ
    zh, j = ex // 8, ex % 8
    core = ex % 2
    near = y + 1 - 2 * (y % 2)
    flip = NY - 1 - y
    yr = near + core * (flip - near)
    yf = flip + core * (near - flip)
    yd = (y + 2) % NY

    def group_dp(h):
        return y * NZ + (NZ - 1 - zl) if h else dp

    def group_ex(h, other):
        return ((1 - zh) if h else zh) * 8 + other

    def dest(h, i):
        return (group_dp(h), group_ex(h, (j + i) % 8))

    def source(h, i):
        return (group_dp(h), group_ex(h, (j + 8 - i) % 8))

    mate = (yr * NZ + zl, ex)
    twin = (yf * NZ + zl, ex)
    right = (dp + 1, ex)
    left = (dp - 1, ex)
    pairs = [(h, i) for h in (1, 0) for i in range(8) if (h, i) != (0, 0)]

    sources = [
        (tok_hbm, tok),
        (og_hbm, og),
        (upw_hbm.at[:, pl.ds(pl.multiple_of(y * 512, 512), 512)], upw.at[:, 0:512]),
        (upw_hbm.at[:, pl.ds(pl.multiple_of(yf * 512, 512), 512)], upw.at[:, 512:1024]),
        (dnw_hbm.at[pl.ds(pl.multiple_of(y * 512, 512), 512), :], dnw.at[0:512, :]),
        (dnw_hbm.at[pl.ds(pl.multiple_of(yf * 512, 512), 512), :], dnw.at[512:1024, :]),
    ]
    loads = [
        pltpu.make_async_copy(src, dst, in_sem.at[n]) for n, (src, dst) in enumerate(sources)
    ]
    for load in loads:
        load.start()

    barrier = pltpu.get_barrier_semaphore()
    for h, i in pairs:
        pl.semaphore_signal(barrier, inc=1, device_id=dest(h, i), device_id_type=MESH)
    for who in (mate, twin):
        pl.semaphore_signal(barrier, inc=1, device_id=who, device_id_type=MESH)

    @pl.when(zl < NZ - 1)
    def _():
        pl.semaphore_signal(barrier, inc=1, device_id=right, device_id_type=MESH)

    @pl.when(zl > 0)
    def _():
        pl.semaphore_signal(barrier, inc=1, device_id=left, device_id_type=MESH)

    ids = id_ref[...]
    ids_row = ids.astype(F32)
    ids_col = to_column(ids_row)
    same = ids_col == ids_row
    before = iota((TOK, TOK), 0) < iota((TOK, TOK), 1)
    after = iota((TOK, TOK), 1) < iota((TOK, TOK), 0)
    pos_row = jnp.sum(jnp.where(same & before, 1.0, 0.0), axis=0, keepdims=True)
    pos_col = jnp.sum(jnp.where(same & after, 1.0, 0.0), axis=1, keepdims=True)

    def slot_of(ident, place):
        mine = zh.astype(F32)
        half = jnp.where(ident >= 8.0, 1.0, 0.0)
        rank = ident - 8.0 * half - j.astype(F32)
        rank = jnp.where(rank < 0.0, rank + 8.0, rank)
        cross = jnp.abs(half - mine)
        return cross * 256.0 + rank * 32.0 + place

    slot_row = slot_of(ids_row, pos_row)
    slot_col = slot_of(ids_col, pos_col)
    gate_row = gate_ref[...].astype(F32)
    gate_col = to_column(gate_row)

    loads[0].wait()
    loads[1].wait()
    og[...] = (gate_col * og[...].astype(F32)).astype(BF)

    pl.semaphore_wait(barrier, 17 + (zl < NZ - 1).astype(jnp.int32) + (zl > 0).astype(jnp.int32))

    def dispatch(h, i):
        return pltpu.make_async_remote_copy(
            src_ref=slots.at[h, i], dst_ref=rows.at[h, i // 4, 0, i % 4],
            send_sem=ds_sem.at[h, i], recv_sem=dr_sem.at[h, i],
            device_id=dest(h, i), device_id_type=MESH,
        )

    def relay(h, i):
        src = slots.at[0, 0] if (h, i) == (0, 0) else rows.at[h, i // 4, 0, i % 4]
        return pltpu.make_async_remote_copy(
            src_ref=src, dst_ref=rows.at[h, i // 4, 1, i % 4],
            send_sem=as_sem.at[h, i], recv_sem=ar_sem.at[h, i],
            device_id=mate, device_id_type=MESH,
        )

    for h in (1, 0):
        place = (iota((TOK, TOK), 0) + TOK * h).astype(F32)
        pick = jnp.where(place == slot_row, 1.0, 0.0).astype(BF)
        slots[h, :, :CAP, :] = dot(pick, tok[...], 1, 0).astype(BF).reshape(8, CAP, D)
        slots[h, :, CAP:, :] = dot(pick, og[...], 1, 0).astype(BF).reshape(8, CAP, D)
        for i in range(8):
            if (h, i) != (0, 0):
                dispatch(h, i).start()
    relay(0, 0).start()
    rows[0, 0, 0, 0] = slots[0, 0]
    for load in loads[2:]:
        load.wait()

    def rows_of(who, h, q):
        return pl.ds((h * 2 + q) * 256 + who * LANES, LANES)

    def forward(h, q):
        here = pl.ds((h * 2 + q) * 256, 256)

        def body(n, acc):
            cols = pl.ds(pl.multiple_of(n * 512, 512), 512)
            feat = rows[h, q, :, :, :CAP, :].reshape(256, D)
            scaled = rows[h, q, :, :, CAP:, :].reshape(256, D)
            pre = dot(feat, upw[:, cols], 1, 0)
            hgrad = dot(scaled, dnw[cols, :], 1, 1)
            cdf = 0.5 * (1.0 + lax.erf(pre * SQRT_HALF))
            hid = (pre * cdf).astype(BF)
            slope = cdf + pre * jnp.exp(-0.5 * pre * pre) * INV_ROOT_TAU
            hidden[here, cols] = hid
            pregrad[here, cols] = (hgrad * slope).astype(BF)
            return acc + jnp.sum(hid.astype(F32) * hgrad, axis=1, keepdims=True)

        total = lax.fori_loop(0, 2, body, jnp.zeros((256, 1), F32))
        eye = iota((CAP, LANES), 0) == iota((CAP, LANES), 1)
        for who, out in ((0, gown), (1, gp)):
            for i in range(4):
                part = total[who * LANES + i * CAP : who * LANES + (i + 1) * CAP, :]
                row = jnp.sum(jnp.where(eye, part, 0.0), axis=0, keepdims=True)
                out[h, 4 * q + i] = jnp.broadcast_to(row, (8, LANES))

    def share_fg(h, q):
        return pltpu.make_async_remote_copy(
            src_ref=fgp.at[h, 4 * q : 4 * q + 4], dst_ref=fgr.at[h, 4 * q : 4 * q + 4],
            send_sem=fs_sem.at[h, q], recv_sem=fr_sem.at[h, q],
            device_id=mate, device_id_type=MESH,
        )

    def share_gate(h, q):
        return pltpu.make_async_remote_copy(
            src_ref=gp.at[h, 4 * q : 4 * q + 4], dst_ref=gr.at[h, 4 * q : 4 * q + 4],
            send_sem=hs_sem.at[h, q], recv_sem=hr_sem.at[h, q],
            device_id=mate, device_id_type=MESH,
        )

    def give_back(h, i):
        return pltpu.make_async_remote_copy(
            src_ref=fgs.at[h, i], dst_ref=back.at[h, i],
            send_sem=bs_sem.at[h, i], recv_sem=br_sem.at[h, i],
            device_id=source(h, i), device_id_type=MESH,
        )

    def give_gate(h, i):
        return pltpu.make_async_remote_copy(
            src_ref=ggs.at[h, i], dst_ref=ggback.at[h, i],
            send_sem=gs_sem.at[h, i], recv_sem=gr_sem.at[h, i],
            device_id=source(h, i), device_id_type=MESH,
        )

    def feature_part(who, h, q, emit):
        here = rows_of(who, h, q)

        @pl.loop(0, D // 512)
        def _(n):
            cols = pl.ds(pl.multiple_of(n * 512, 512), 512)
            emit(cols, dot(pregrad[here, :], upw[cols, :], 1, 1).reshape(4, CAP, 512))

    def mate_part(h, q):
        def emit(cols, v):
            fgp[h, 4 * q : 4 * q + 4, :, cols] = v.astype(BF)

        feature_part(1, h, q, emit)
        share_fg(h, q).start()
        share_gate(h, q).start()

    def finish(h, q):
        some = slice(4 * q, 4 * q + 4)
        share_fg(h, q).wait_recv()
        share_gate(h, q).wait_recv()

        def emit(cols, v):
            fgs[h, some, :, cols] = (v + fgr[h, some, :, cols].astype(F32)).astype(BF)

        feature_part(0, h, q, emit)
        ggs[h, some] = gown[h, some] + gr[h, some]
        for i in range(4 * q, 4 * q + 4):
            if (h, i) == (0, 0):
                back[0, 0] = fgs[0, 0]
                ggback[0, 0] = ggs[0, 0]
            else:
                give_back(h, i).start()
                give_gate(h, i).start()

    last = None
    for h, q in ((0, 0), (0, 1), (1, 0), (1, 1)):
        for i in range(4 * q, 4 * q + 4):
            if (h, i) != (0, 0):
                dispatch(h, i).wait_recv()
                relay(h, i).start()
        if last is not None:
            finish(*last)
        for i in range(4 * q, 4 * q + 4):
            relay(h, i).wait_recv()
        forward(h, q)
        mate_part(h, q)
        last = (h, q)

    def up_part(first, second, emit):
        @pl.loop(0, 2)
        def _(c):
            chunk = first + c * (second - first)
            feats = pl.ds(pl.multiple_of(chunk * 256, 256), 256)
            lhs = rows[:, :, :, :, :CAP, feats].reshape(1024, 256).T
            for n in range(2):
                emit(c, n, dot(lhs, pregrad[:, n * 512 : n * 512 + 512], 1, 0))

    def down_part(half, emit):
        @pl.loop(0, 2)
        def _(m):
            feats = pl.ds(pl.multiple_of(half * 512 + m * 256, 256), 256)
            lhs = hidden[:, feats].T
            for n in range(2):
                rhs = rows[:, :, :, :, CAP:, n * 512 : n * 512 + 512].reshape(1024, 512)
                emit(m, n, dot(lhs, rhs, 1, 0))

    def ysend(t, k):
        src, dst = ((su_out, su_in), (sd_out, sd_in))[t]
        return pltpu.make_async_remote_copy(
            src_ref=src.at[k], dst_ref=dst.at[k],
            send_sem=ys_sem.at[t, k], recv_sem=yr_sem.at[t, k],
            device_id=twin, device_id_type=MESH,
        )

    low = 1 - zl // 2

    def block(n):
        k = n // 2 + (n % 2) * (3 - 2 * (n // 2))
        return k + low * (3 - 2 * k)

    def emit_up_out(c, n, v):
        for k in range(4):
            su_out[k, c, :, (1 - n) * 512 : (2 - n) * 512] = v[64 * k : 64 * k + 64].astype(BF)

    def emit_up_own(c, n, v):
        for k in range(4):
            pu[k, c, :, n * 512 : n * 512 + 512] = v[64 * k : 64 * k + 64]

    def emit_down_out(m, n, v):
        for s in range(2):
            sd_out[2 * m + s, :, n * 512 : n * 512 + 512] = v[128 * s : 128 * s + 128].astype(BF)

    def emit_down_own(m, n, v):
        for s in range(2):
            pd[2 * m + s, :, n * 512 : n * 512 + 512] = v[128 * s : 128 * s + 128]

    zrefs = ((zu, zlu, zru), (zd, zld, zrd))

    def zright(t, k):
        src, dst, _ = zrefs[t]
        return pltpu.make_async_remote_copy(
            src_ref=src.at[k], dst_ref=dst.at[k],
            send_sem=zs_sem.at[t, k], recv_sem=zl_sem.at[t, k],
            device_id=right, device_id_type=MESH,
        )

    def zleft(t, k):
        src, _, dst = zrefs[t]
        return pltpu.make_async_remote_copy(
            src_ref=src.at[k], dst_ref=dst.at[k],
            send_sem=zs_sem.at[t, k], recv_sem=zr_sem.at[t, k],
            device_id=left, device_id_type=MESH,
        )

    def line(t, k, total, final):
        out, from_left, from_right = zrefs[t]

        @pl.when(zl == k)
        def _():
            final[...] = total[...]

        @pl.when((zl < k) & (zl == 0))
        def _():
            out[k] = total[...].astype(BF)

        @pl.when((zl < k) & (zl > 0))
        def _():
            zright(t, k).wait_recv()
            out[k] = (total[...] + from_left[k].astype(F32)).astype(BF)

        @pl.when(zl < k)
        def _():
            zright(t, k).start()

        @pl.when((zl > k) & (zl == NZ - 1))
        def _():
            out[k] = total[...].astype(BF)

        @pl.when((zl > k) & (zl < NZ - 1))
        def _():
            zleft(t, k).wait_recv()
            out[k] = (total[...] + from_right[k].astype(F32)).astype(BF)

        @pl.when(zl > k)
        def _():
            zleft(t, k).start()

    def step(t, n):
        k = block(n)
        own, came = ((pu, su_in), (pd, sd_in))[t]
        ysend(t, k).wait_recv()
        own[k] = own[k] + came[k].astype(F32)
        line(t, k, own.at[k], (fu, fd)[t])

    edge = (zl == 0) | (zl == NZ - 1)

    up_part(yf, yd, emit_up_out)
    for n in range(4):
        ysend(0, block(n)).start()
    up_part(y, yr, emit_up_own)

    @pl.when(edge)
    def _():
        step(0, 0)

    finish(*last)
    down_part(1, emit_down_out)
    for n in range(4):
        ysend(1, block(n)).start()

    @pl.when(jnp.logical_not(edge))
    def _():
        step(0, 0)

    down_part(0, emit_down_own)

    @pl.loop(1, 4)
    def _(n):
        step(0, n)

    def settle(t, final):
        _, from_left, from_right = zrefs[t]

        @pl.when(zl > 0)
        def _():
            zright(t, zl).wait_recv()
            final[...] = final[...] + from_left[zl].astype(F32)

        @pl.when(zl < NZ - 1)
        def _():
            zleft(t, zl).wait_recv()
            final[...] = final[...] + from_right[zl].astype(F32)

    for n in range(2):
        step(1, n)
    settle(0, fu)
    swap = pltpu.make_async_remote_copy(
        src_ref=fu.at[1], dst_ref=xu,
        send_sem=xs_sem.at[0], recv_sem=xr_sem.at[0],
        device_id=mate, device_id_type=MESH,
    )
    swap.start()
    for n in range(2, 4):
        step(1, n)

    for h, i in pairs:
        give_back(h, i).wait_recv()
        give_gate(h, i).wait_recv()
    spread = jnp.where(iota((TOK, 512), 1).astype(F32) == slot_col, 1.0, 0.0).astype(BF)

    @pl.loop(0, D // 512)
    def _(n):
        cols = pl.ds(pl.multiple_of(n * 512, 512), 512)
        tg_ref[:, cols] = dot(spread, back[:, :, :, cols].reshape(512, 512), 1, 0).astype(BF)

    lane = iota((TOK, LANES), 1).astype(F32)
    gate_sum = jnp.zeros((TOK, LANES), F32)
    for h in range(2):
        for i in range(8):
            base = float(h * 256 + i * CAP)
            hit = (lane < float(CAP)) & (lane + base == slot_col)
            gate_sum += jnp.where(hit, ggback[h, i, 0:1, :], 0.0)
    gate_total = jnp.sum(gate_sum, axis=1, keepdims=True) / gate_col
    eye = iota((TOK, TOK), 0) == iota((TOK, TOK), 1)
    gg_ref[...] = jnp.sum(jnp.where(eye, gate_total, 0.0), axis=0, keepdims=True).astype(BF)

    scale = 1.0 / (NY * NZ)

    def ff_chunk(c):
        return pl.ds(pl.multiple_of(c * 512, 512), 512)

    swap.wait_recv()
    ug_ref[:, ff_chunk(y)] = fu[0, :, 0:512] * scale
    ug_ref[:, ff_chunk(yf)] = fu[0, :, 512:1024] * scale
    ug_ref[:, ff_chunk(yr)] = xu[:, 0:512] * scale
    ug_ref[:, ff_chunk(yd)] = xu[:, 512:1024] * scale
    settle(1, fd)
    dg_ref[...] = fd[...] * scale

    swap.wait_send()
    relay(0, 0).wait_send()
    for h, i in pairs:
        dispatch(h, i).wait_send()
        relay(h, i).wait_send()
        give_back(h, i).wait_send()
        give_gate(h, i).wait_send()
    for h in range(2):
        for q in range(2):
            share_fg(h, q).wait_send()
            share_gate(h, q).wait_send()

    @pl.loop(0, 4)
    def _(k):
        ysend(0, k).wait_send()
        ysend(1, k).wait_send()

        @pl.when(zl != k)
        def _():
            zright(0, k).wait_send()
            zright(1, k).wait_send()


def tail(tg_in, gg_in, ug_in, dg_in, tg_out, gg_out, ug_out, dg_out, tg, ug, dg, sem_in, sem_out):
    moves = ((tg_in, tg, tg_out), (ug_in, ug, ug_out), (dg_in, dg, dg_out))
    ins = [pltpu.make_async_copy(a, b, sem_in.at[n]) for n, (a, b, _) in enumerate(moves)]
    outs = [pltpu.make_async_copy(b, c, sem_out.at[n]) for n, (_, b, c) in enumerate(moves)]
    for copy in ins:
        copy.start()
    gg_out[...] = gg_in[...]
    for arrive, leave in zip(ins, outs):
        arrive.wait()
        leave.start()
    for leave in outs:
        leave.wait()


def per_device(tokens, out_grad, gate_prob, expert_id, up_weight, down_weight):
    any_spec = pl.BlockSpec(memory_space=pl.ANY)
    vmem = pl.BlockSpec(memory_space=pltpu.VMEM)
    up_blocks = pltpu.VMEM((4, 2, 64, 1024), BF)
    down_blocks = pltpu.VMEM((4, 128, D), BF)
    grads = pltpu.VMEM((2, 8, CAP, D), BF)
    gates = pltpu.VMEM((2, 8, 8, LANES), F32)
    dma = pltpu.SemaphoreType.DMA
    tg, gg, ug, dg = pl.pallas_call(
        kernel,
        out_shape=(
            jax.ShapeDtypeStruct((TOK, D), BF),
            jax.ShapeDtypeStruct((1, TOK), BF),
            jax.ShapeDtypeStruct((64, FF), F32),
            jax.ShapeDtypeStruct((128, D), F32),
        ),
        in_specs=[any_spec, any_spec, vmem, vmem, any_spec, any_spec],
        out_specs=(vmem, vmem, vmem, vmem),
        scratch_shapes=[
            pltpu.VMEM((TOK, D), BF),
            pltpu.VMEM((TOK, D), BF),
            pltpu.VMEM((D, 1024), BF),
            pltpu.VMEM((1024, D), BF),
            pltpu.VMEM((2, 8, 2 * CAP, D), BF),
            pltpu.VMEM((2, 2, 2, 4, 2 * CAP, D), BF),
            pltpu.VMEM((1024, 1024), BF),
            pltpu.VMEM((1024, 1024), BF),
            grads, grads, grads, grads,
            gates, gates, gates, gates, gates,
            up_blocks, down_blocks, up_blocks, down_blocks, up_blocks, down_blocks,
            up_blocks, down_blocks, up_blocks, down_blocks,
            pltpu.VMEM((2, 64, 1024), F32),
            pltpu.VMEM((128, D), F32),
            pltpu.VMEM((64, 1024), F32),
            pltpu.VMEM((4, 2, 64, 1024), F32),
            pltpu.VMEM((4, 128, D), F32),
            dma((6,)),
            dma((2, 8)), dma((2, 8)), dma((2, 8)), dma((2, 8)),
            dma((2, 2)), dma((2, 2)), dma((2, 2)), dma((2, 2)),
            dma((2, 8)), dma((2, 8)), dma((2, 8)), dma((2, 8)),
            dma((2, 4)), dma((2, 4)), dma((2, 4)), dma((2, 4)), dma((2, 4)), dma((1,)), dma((1,)),
        ],
        compiler_params=pltpu.CompilerParams(
            collective_id=0, has_side_effects=True, vmem_limit_bytes=60 * 1024 * 1024
        ),
    )(
        tokens,
        out_grad,
        gate_prob.reshape(1, TOK),
        expert_id.reshape(1, TOK),
        up_weight[0],
        down_weight[0],
    )
    tg, gg, ug, dg = pl.pallas_call(
        tail,
        out_shape=(
            jax.ShapeDtypeStruct((TOK, D), BF),
            jax.ShapeDtypeStruct((1, TOK), BF),
            jax.ShapeDtypeStruct((64, FF), F32),
            jax.ShapeDtypeStruct((128, D), F32),
        ),
        in_specs=[any_spec, vmem, any_spec, any_spec],
        out_specs=(any_spec, vmem, any_spec, any_spec),
        scratch_shapes=[
            pltpu.VMEM((TOK, D), BF),
            pltpu.VMEM((64, FF), F32),
            pltpu.VMEM((128, D), F32),
            dma((3,)),
            dma((3,)),
        ],
    )(tg, gg, ug, dg)
    return tg, gg.reshape(TOK), ug[None], dg[None]


def solution(mesh):
    return jax.shard_map(
        per_device,
        mesh=mesh,
        in_specs=(
            P(("dp", "expert"), None),
            P(("dp", "expert"), None),
            P(("dp", "expert")),
            P(("dp", "expert")),
            P("expert", None, None),
            P("expert", None, None),
        ),
        out_specs=(
            P(("dp", "expert"), None),
            P(("dp", "expert")),
            P("expert", "dp", None),
            P("expert", "dp", None),
        ),
        check_vma=False,
    )
```

```python
import jax
import jax.numpy as jnp
from jax import lax
from jax.experimental import pallas as pl
from jax.experimental.pallas import tpu as pltpu
from jax.sharding import PartitionSpec as P

MESH = pl.DeviceIdType.MESH
SQRT_HALF = 0.7071067811865476
INV_ROOT_TAU = 0.3989422804014327
BF = jnp.bfloat16
F32 = jnp.float32
D = 1024
FF = 2048
TOK = 256
CAP = 32
NY = 4
NZ = 4
LANES = 128
AWAY = (0, 1, 2, 3, 6, 7, 4, 5)


def dot(a, b, ca, cb):
    return lax.dot_general(a, b, (((ca,), (cb,)), ((), ())), preferred_element_type=F32)


def iota(shape, axis):
    return lax.broadcasted_iota(jnp.int32, shape, axis)


def to_column(row):
    n = row.shape[1]
    eye = iota((n, n), 0) == iota((n, n), 1)
    return jnp.sum(jnp.where(eye, row, 0.0), axis=1, keepdims=True)


def kernel(
    tok_hbm, og_hbm, gate_ref, id_ref, upw_hbm, dnw_hbm,
    tg_ref, gg_ref, ug_ref, dg_ref,
    tok, og, upw, dnw, slots, rows, hidden, pregrad, fgp, fgr, fgs, back,
    gown, gp, gr, ggs, ggback,
    su_out, sd_out, su_in, sd_in, zu, zd, zlu, zld, zru, zrd, fu, fd, xu, pu, pd,
    in_sem, ds_sem, dr_sem, as_sem, ar_sem, fs_sem, fr_sem, hs_sem, hr_sem,
    bs_sem, br_sem, gs_sem, gr_sem, ys_sem, yr_sem, zs_sem, zl_sem, zr_sem, xs_sem, xr_sem,
):
    dp = lax.axis_index("dp")
    ex = lax.axis_index("expert")
    y, zl = dp // NZ, dp % NZ
    zh, j = ex // 8, ex % 8
    core = ex % 2
    near = y + 1 - 2 * (y % 2)
    flip = NY - 1 - y
    yr = near + core * (flip - near)
    yf = flip + core * (near - flip)
    yd = (y + 2) % NY

    def group_dp(h):
        return y * NZ + (NZ - 1 - zl) if h else dp

    def group_ex(h, other):
        return ((1 - zh) if h else zh) * 8 + other

    def dest(h, i):
        return (group_dp(h), group_ex(h, (j + AWAY[i]) % 8))

    def source(h, i):
        return (group_dp(h), group_ex(h, (j + 8 - AWAY[i]) % 8))

    mate = (yr * NZ + zl, ex)
    twin = (yf * NZ + zl, ex)
    right = (dp + 1, ex)
    left = (dp - 1, ex)
    pairs = [(h, i) for h in (1, 0) for i in range(8) if (h, i) != (0, 0)]

    sources = [
        (tok_hbm, tok),
        (og_hbm, og),
        (upw_hbm.at[:, pl.ds(pl.multiple_of(y * 512, 512), 512)], upw.at[:, 0:512]),
        (upw_hbm.at[:, pl.ds(pl.multiple_of(yf * 512, 512), 512)], upw.at[:, 512:1024]),
        (dnw_hbm.at[pl.ds(pl.multiple_of(y * 512, 512), 512), :], dnw.at[0:512, :]),
        (dnw_hbm.at[pl.ds(pl.multiple_of(yf * 512, 512), 512), :], dnw.at[512:1024, :]),
    ]
    loads = [
        pltpu.make_async_copy(src, dst, in_sem.at[n]) for n, (src, dst) in enumerate(sources)
    ]
    for load in loads:
        load.start()

    barrier = pltpu.get_barrier_semaphore()
    for h, i in pairs:
        pl.semaphore_signal(barrier, inc=1, device_id=dest(h, i), device_id_type=MESH)
    for who in (mate, twin):
        pl.semaphore_signal(barrier, inc=1, device_id=who, device_id_type=MESH)

    @pl.when(zl < NZ - 1)
    def _():
        pl.semaphore_signal(barrier, inc=1, device_id=right, device_id_type=MESH)

    @pl.when(zl > 0)
    def _():
        pl.semaphore_signal(barrier, inc=1, device_id=left, device_id_type=MESH)

    ids = id_ref[...]
    ids_row = ids.astype(F32)
    ids_col = to_column(ids_row)
    same = ids_col == ids_row
    before = iota((TOK, TOK), 0) < iota((TOK, TOK), 1)
    after = iota((TOK, TOK), 1) < iota((TOK, TOK), 0)
    pos_row = jnp.sum(jnp.where(same & before, 1.0, 0.0), axis=0, keepdims=True)
    pos_col = jnp.sum(jnp.where(same & after, 1.0, 0.0), axis=1, keepdims=True)

    def slot_of(ident, place):
        mine = zh.astype(F32)
        half = jnp.where(ident >= 8.0, 1.0, 0.0)
        rank = ident - 8.0 * half - j.astype(F32)
        rank = jnp.where(rank < 0.0, rank + 8.0, rank)
        rank = rank + jnp.where(rank >= 6.0, -2.0, jnp.where(rank >= 4.0, 2.0, 0.0))
        cross = jnp.abs(half - mine)
        return cross * 256.0 + rank * 32.0 + place

    slot_row = slot_of(ids_row, pos_row)
    slot_col = slot_of(ids_col, pos_col)
    gate_row = gate_ref[...].astype(F32)
    gate_col = to_column(gate_row)

    loads[0].wait()
    loads[1].wait()
    og[...] = (gate_col * og[...].astype(F32)).astype(BF)

    pl.semaphore_wait(barrier, 17 + (zl < NZ - 1).astype(jnp.int32) + (zl > 0).astype(jnp.int32))

    def dispatch(h, i):
        return pltpu.make_async_remote_copy(
            src_ref=slots.at[h, i], dst_ref=rows.at[h, i // 2, 0, i % 2],
            send_sem=ds_sem.at[h, i], recv_sem=dr_sem.at[h, i],
            device_id=dest(h, i), device_id_type=MESH,
        )

    def relay(h, i):
        src = slots.at[0, 0] if (h, i) == (0, 0) else rows.at[h, i // 2, 0, i % 2]
        return pltpu.make_async_remote_copy(
            src_ref=src, dst_ref=rows.at[h, i // 2, 1, i % 2],
            send_sem=as_sem.at[h, i], recv_sem=ar_sem.at[h, i],
            device_id=mate, device_id_type=MESH,
        )

    for h in (1, 0):
        place = (iota((TOK, TOK), 0) + TOK * h).astype(F32)
        pick = jnp.where(place == slot_row, 1.0, 0.0).astype(BF)
        slots[h, :, :CAP, :] = dot(pick, tok[...], 1, 0).astype(BF).reshape(8, CAP, D)
        slots[h, :, CAP:, :] = dot(pick, og[...], 1, 0).astype(BF).reshape(8, CAP, D)
        for i in range(8):
            if (h, i) != (0, 0):
                dispatch(h, i).start()
    relay(0, 0).start()
    rows[0, 0, 0, 0] = slots[0, 0]
    for load in loads[2:]:
        load.wait()

    def forward(h, first, count):
        size = count * 2 * CAP
        here = pl.ds((h * 8 + first) * 2 * CAP, size)
        some = slice(first // 2, (first + count) // 2)
        total = jnp.zeros((size, 1), F32)
        for n in range(2):
            cols = slice(n * 512, n * 512 + 512)
            feat = rows[h, some, :, :, :CAP, :].reshape(size, D)
            scaled = rows[h, some, :, :, CAP:, :].reshape(size, D)
            pre = dot(feat, upw[:, cols], 1, 0)
            hgrad = dot(scaled, dnw[cols, :], 1, 1)
            cdf = 0.5 * (1.0 + lax.erf(pre * SQRT_HALF))
            hid = (pre * cdf).astype(BF)
            slope = cdf + pre * jnp.exp(-0.5 * pre * pre) * INV_ROOT_TAU
            hidden[here, cols] = hid
            pregrad[here, cols] = (hgrad * slope).astype(BF)
            total += jnp.sum(hid.astype(F32) * hgrad, axis=1, keepdims=True)
        eye = iota((CAP, LANES), 0) == iota((CAP, LANES), 1)
        for pair in range(count // 2):
            for who, out in ((0, gown), (1, gp)):
                for i in range(2):
                    start = (pair * 4 + who * 2 + i) * CAP
                    part = total[start : start + CAP, :]
                    row = jnp.sum(jnp.where(eye, part, 0.0), axis=0, keepdims=True)
                    out[h, first + 2 * pair + i] = jnp.broadcast_to(row, (8, LANES))

    def share_fg(h, q):
        return pltpu.make_async_remote_copy(
            src_ref=fgp.at[h, 4 * q : 4 * q + 4], dst_ref=fgr.at[h, 4 * q : 4 * q + 4],
            send_sem=fs_sem.at[h, q], recv_sem=fr_sem.at[h, q],
            device_id=mate, device_id_type=MESH,
        )

    def share_gate(h, q):
        return pltpu.make_async_remote_copy(
            src_ref=gp.at[h, 4 * q : 4 * q + 4], dst_ref=gr.at[h, 4 * q : 4 * q + 4],
            send_sem=hs_sem.at[h, q], recv_sem=hr_sem.at[h, q],
            device_id=mate, device_id_type=MESH,
        )

    def give_back(h, i):
        return pltpu.make_async_remote_copy(
            src_ref=fgs.at[h, i], dst_ref=back.at[h, i],
            send_sem=bs_sem.at[h, i], recv_sem=br_sem.at[h, i],
            device_id=source(h, i), device_id_type=MESH,
        )

    def give_gate(h, i):
        return pltpu.make_async_remote_copy(
            src_ref=ggs.at[h, i], dst_ref=ggback.at[h, i],
            send_sem=gs_sem.at[h, i], recv_sem=gr_sem.at[h, i],
            device_id=source(h, i), device_id_type=MESH,
        )

    def feature_part(who, h, q, emit):
        @pl.loop(0, D // 512)
        def _(n):
            cols = pl.ds(pl.multiple_of(n * 512, 512), 512)
            base = (h * 8 + 4 * q) * 2 * CAP + who * 2 * CAP
            lhs = jnp.concatenate(
                [pregrad[pl.ds(base + p * 4 * CAP, 2 * CAP), :] for p in range(2)], axis=0
            )
            emit(cols, dot(lhs, upw[cols, :], 1, 1).reshape(4, CAP, 512))

    def mate_part(h, q):
        def emit(cols, v):
            fgp[h, 4 * q : 4 * q + 4, :, cols] = v.astype(BF)

        feature_part(1, h, q, emit)
        share_fg(h, q).start()
        share_gate(h, q).start()

    def finish(h, q):
        some = slice(4 * q, 4 * q + 4)
        share_fg(h, q).wait_recv()
        share_gate(h, q).wait_recv()

        def emit(cols, v):
            fgs[h, some, :, cols] = (v + fgr[h, some, :, cols].astype(F32)).astype(BF)

        feature_part(0, h, q, emit)
        ggs[h, some] = gown[h, some] + gr[h, some]
        for i in range(4 * q, 4 * q + 4):
            if (h, i) == (0, 0):
                back[0, 0] = fgs[0, 0]
                ggback[0, 0] = ggs[0, 0]
            else:
                give_back(h, i).start()
                give_gate(h, i).start()

    last = None
    for h, q in ((0, 0), (0, 1), (1, 0), (1, 1)):
        final = (h, q) == (1, 1)
        for first, count in ((4 * q, 2), (4 * q + 2, 2)) if final else ((4 * q, 4),):
            for i in range(first, first + count):
                if (h, i) != (0, 0):
                    dispatch(h, i).wait_recv()
                    relay(h, i).start()
            if last is not None and first == 4 * q:
                finish(*last)
            for i in range(first, first + count):
                relay(h, i).wait_recv()
            forward(h, first, count)
        if not final:
            mate_part(h, q)
        last = (h, q)

    low = 1 - zl // 2

    def block(n):
        k = n // 2 + (n % 2) * (3 - 2 * (n // 2))
        return k + low * (3 - 2 * k)

    def up_part(first, second, emit):
        @pl.loop(0, 2)
        def _(c):
            chunk = first + c * (second - first)
            feats = pl.ds(pl.multiple_of(chunk * 256, 256), 256)
            lhs = rows[:, :, :, :, :CAP, feats].reshape(1024, 256).T
            for n in range(2):
                emit(c, n, dot(lhs, pregrad[:, n * 512 : n * 512 + 512], 1, 0))

    def down_part(half, n0, emit):
        blocks = (block(n0), block(n0 + 1))
        lhs = jnp.concatenate(
            [
                hidden[:, pl.ds(pl.multiple_of(half * 512 + k * LANES, LANES), LANES)].T
                for k in blocks
            ],
            axis=0,
        )
        for n in range(2):
            rhs = rows[:, :, :, :, CAP:, n * 512 : n * 512 + 512].reshape(1024, 512)
            v = dot(lhs, rhs, 1, 0)
            emit(blocks[0], n, v[:LANES])
            emit(blocks[1], n, v[LANES:])

    def ysend(t, k):
        src, dst = ((su_out, su_in), (sd_out, sd_in))[t]
        return pltpu.make_async_remote_copy(
            src_ref=src.at[k], dst_ref=dst.at[k],
            send_sem=ys_sem.at[t, k], recv_sem=yr_sem.at[t, k],
            device_id=twin, device_id_type=MESH,
        )

    def emit_up_out(c, n, v):
        for k in range(4):
            su_out[k, c, :, (1 - n) * 512 : (2 - n) * 512] = v[64 * k : 64 * k + 64].astype(BF)

    def emit_up_own(c, n, v):
        for k in range(4):
            pu[k, c, :, n * 512 : n * 512 + 512] = v[64 * k : 64 * k + 64]

    def emit_down_out(k, n, v):
        sd_out[k, :, n * 512 : n * 512 + 512] = v.astype(BF)

    def emit_down_own(k, n, v):
        pd[k, :, n * 512 : n * 512 + 512] = v

    zrefs = ((zu, zlu, zru), (zd, zld, zrd))

    def zright(t, k):
        src, dst, _ = zrefs[t]
        return pltpu.make_async_remote_copy(
            src_ref=src.at[k], dst_ref=dst.at[k],
            send_sem=zs_sem.at[t, k], recv_sem=zl_sem.at[t, k],
            device_id=right, device_id_type=MESH,
        )

    def zleft(t, k):
        src, _, dst = zrefs[t]
        return pltpu.make_async_remote_copy(
            src_ref=src.at[k], dst_ref=dst.at[k],
            send_sem=zs_sem.at[t, k], recv_sem=zr_sem.at[t, k],
            device_id=left, device_id_type=MESH,
        )

    def line(t, k, total, final):
        out, from_left, from_right = zrefs[t]

        @pl.when(zl == k)
        def _():
            final[...] = total[...]

        @pl.when((zl < k) & (zl == 0))
        def _():
            out[k] = total[...].astype(BF)

        @pl.when((zl < k) & (zl > 0))
        def _():
            zright(t, k).wait_recv()
            out[k] = (total[...] + from_left[k].astype(F32)).astype(BF)

        @pl.when(zl < k)
        def _():
            zright(t, k).start()

        @pl.when((zl > k) & (zl == NZ - 1))
        def _():
            out[k] = total[...].astype(BF)

        @pl.when((zl > k) & (zl < NZ - 1))
        def _():
            zleft(t, k).wait_recv()
            out[k] = (total[...] + from_right[k].astype(F32)).astype(BF)

        @pl.when(zl > k)
        def _():
            zleft(t, k).start()

    def step(t, n):
        k = block(n)
        own, came = ((pu, su_in), (pd, sd_in))[t]
        ysend(t, k).wait_recv()
        own[k] = own[k] + came[k].astype(F32)
        line(t, k, own.at[k], (fu, fd)[t])

    edge = (zl == 0) | (zl == NZ - 1)

    down_part(1, 0, emit_down_out)
    for n in range(2):
        ysend(1, block(n)).start()
    down_part(0, 0, emit_down_own)
    mate_part(1, 1)

    @pl.when(edge)
    def _():
        step(1, 0)

    up_part(yf, yd, emit_up_out)
    for n in range(4):
        ysend(0, block(n)).start()
    finish(*last)
    up_part(y, yr, emit_up_own)

    @pl.when(jnp.logical_not(edge))
    def _():
        step(1, 0)

    step(1, 1)
    step(0, 0)
    down_part(1, 2, emit_down_out)
    for n in range(2, 4):
        ysend(1, block(n)).start()
    down_part(0, 2, emit_down_own)

    @pl.loop(1, 4)
    def _(n):
        step(0, n)

    step(1, 2)

    def settle(t, final):
        _, from_left, from_right = zrefs[t]

        @pl.when(zl > 0)
        def _():
            zright(t, zl).wait_recv()
            final[...] = final[...] + from_left[zl].astype(F32)

        @pl.when(zl < NZ - 1)
        def _():
            zleft(t, zl).wait_recv()
            final[...] = final[...] + from_right[zl].astype(F32)

    settle(0, fu)
    swap = pltpu.make_async_remote_copy(
        src_ref=fu.at[1], dst_ref=xu,
        send_sem=xs_sem.at[0], recv_sem=xr_sem.at[0],
        device_id=mate, device_id_type=MESH,
    )
    swap.start()
    step(1, 3)

    for h, i in pairs:
        give_back(h, i).wait_recv()
        give_gate(h, i).wait_recv()
    spread = jnp.where(iota((TOK, 512), 1).astype(F32) == slot_col, 1.0, 0.0).astype(BF)

    @pl.loop(0, D // 512)
    def _(n):
        cols = pl.ds(pl.multiple_of(n * 512, 512), 512)
        tg_ref[:, cols] = dot(spread, back[:, :, :, cols].reshape(512, 512), 1, 0).astype(BF)

    lane = iota((TOK, LANES), 1).astype(F32)
    gate_sum = jnp.zeros((TOK, LANES), F32)
    for h in range(2):
        for i in range(8):
            base = float(h * 256 + i * CAP)
            hit = (lane < float(CAP)) & (lane + base == slot_col)
            gate_sum += jnp.where(hit, ggback[h, i, 0:1, :], 0.0)
    gate_total = jnp.sum(gate_sum, axis=1, keepdims=True) / gate_col
    eye = iota((TOK, TOK), 0) == iota((TOK, TOK), 1)
    gg_ref[...] = jnp.sum(jnp.where(eye, gate_total, 0.0), axis=0, keepdims=True).astype(BF)

    scale = 1.0 / (NY * NZ)

    def ff_chunk(c):
        return pl.ds(pl.multiple_of(c * 512, 512), 512)

    swap.wait_recv()
    ug_ref[:, ff_chunk(y)] = fu[0, :, 0:512] * scale
    ug_ref[:, ff_chunk(yf)] = fu[0, :, 512:1024] * scale
    ug_ref[:, ff_chunk(yr)] = xu[:, 0:512] * scale
    ug_ref[:, ff_chunk(yd)] = xu[:, 512:1024] * scale
    settle(1, fd)
    dg_ref[...] = fd[...] * scale

    swap.wait_send()
    relay(0, 0).wait_send()
    for h, i in pairs:
        dispatch(h, i).wait_send()
        relay(h, i).wait_send()
        give_back(h, i).wait_send()
        give_gate(h, i).wait_send()
    for h in range(2):
        for q in range(2):
            share_fg(h, q).wait_send()
            share_gate(h, q).wait_send()

    @pl.loop(0, 4)
    def _(k):
        ysend(0, k).wait_send()
        ysend(1, k).wait_send()

        @pl.when(zl != k)
        def _():
            zright(0, k).wait_send()
            zright(1, k).wait_send()


def tail(tg_in, gg_in, ug_in, dg_in, tg_out, gg_out, ug_out, dg_out, tg, ug, dg, sem_in, sem_out):
    moves = ((tg_in, tg, tg_out), (ug_in, ug, ug_out), (dg_in, dg, dg_out))
    ins = [pltpu.make_async_copy(a, b, sem_in.at[n]) for n, (a, b, _) in enumerate(moves)]
    outs = [pltpu.make_async_copy(b, c, sem_out.at[n]) for n, (_, b, c) in enumerate(moves)]
    for copy in ins:
        copy.start()
    gg_out[...] = gg_in[...]
    for arrive, leave in zip(ins, outs):
        arrive.wait()
        leave.start()
    for leave in outs:
        leave.wait()


def per_device(tokens, out_grad, gate_prob, expert_id, up_weight, down_weight):
    any_spec = pl.BlockSpec(memory_space=pl.ANY)
    vmem = pl.BlockSpec(memory_space=pltpu.VMEM)
    up_blocks = pltpu.VMEM((4, 2, 64, 1024), BF)
    down_blocks = pltpu.VMEM((4, 128, D), BF)
    grads = pltpu.VMEM((2, 8, CAP, D), BF)
    gates = pltpu.VMEM((2, 8, 8, LANES), F32)
    dma = pltpu.SemaphoreType.DMA
    tg, gg, ug, dg = pl.pallas_call(
        kernel,
        out_shape=(
            jax.ShapeDtypeStruct((TOK, D), BF),
            jax.ShapeDtypeStruct((1, TOK), BF),
            jax.ShapeDtypeStruct((64, FF), F32),
            jax.ShapeDtypeStruct((128, D), F32),
        ),
        in_specs=[any_spec, any_spec, vmem, vmem, any_spec, any_spec],
        out_specs=(vmem, vmem, vmem, vmem),
        scratch_shapes=[
            pltpu.VMEM((TOK, D), BF),
            pltpu.VMEM((TOK, D), BF),
            pltpu.VMEM((D, 1024), BF),
            pltpu.VMEM((1024, D), BF),
            pltpu.VMEM((2, 8, 2 * CAP, D), BF),
            pltpu.VMEM((2, 4, 2, 2, 2 * CAP, D), BF),
            pltpu.VMEM((1024, 1024), BF),
            pltpu.VMEM((1024, 1024), BF),
            grads, grads, grads, grads,
            gates, gates, gates, gates, gates,
            up_blocks, down_blocks, up_blocks, down_blocks, up_blocks, down_blocks,
            up_blocks, down_blocks, up_blocks, down_blocks,
            pltpu.VMEM((2, 64, 1024), F32),
            pltpu.VMEM((128, D), F32),
            pltpu.VMEM((64, 1024), F32),
            pltpu.VMEM((4, 2, 64, 1024), F32),
            pltpu.VMEM((4, 128, D), F32),
            dma((6,)),
            dma((2, 8)), dma((2, 8)), dma((2, 8)), dma((2, 8)),
            dma((2, 2)), dma((2, 2)), dma((2, 2)), dma((2, 2)),
            dma((2, 8)), dma((2, 8)), dma((2, 8)), dma((2, 8)),
            dma((2, 4)), dma((2, 4)), dma((2, 4)), dma((2, 4)), dma((2, 4)), dma((1,)), dma((1,)),
        ],
        compiler_params=pltpu.CompilerParams(
            collective_id=0, has_side_effects=True, vmem_limit_bytes=60 * 1024 * 1024
        ),
    )(
        tokens,
        out_grad,
        gate_prob.reshape(1, TOK),
        expert_id.reshape(1, TOK),
        up_weight[0],
        down_weight[0],
    )
    tg, gg, ug, dg = pl.pallas_call(
        tail,
        out_shape=(
            jax.ShapeDtypeStruct((TOK, D), BF),
            jax.ShapeDtypeStruct((1, TOK), BF),
            jax.ShapeDtypeStruct((64, FF), F32),
            jax.ShapeDtypeStruct((128, D), F32),
        ),
        in_specs=[any_spec, vmem, any_spec, any_spec],
        out_specs=(any_spec, vmem, any_spec, any_spec),
        scratch_shapes=[
            pltpu.VMEM((TOK, D), BF),
            pltpu.VMEM((64, FF), F32),
            pltpu.VMEM((128, D), F32),
            dma((3,)),
            dma((3,)),
        ],
    )(tg, gg, ug, dg)
    return tg, gg.reshape(TOK), ug[None], dg[None]


def solution(mesh):
    return jax.shard_map(
        per_device,
        mesh=mesh,
        in_specs=(
            P(("dp", "expert"), None),
            P(("dp", "expert"), None),
            P(("dp", "expert")),
            P(("dp", "expert")),
            P("expert", None, None),
            P("expert", None, None),
        ),
        out_specs=(
            P(("dp", "expert"), None),
            P(("dp", "expert")),
            P("expert", "dp", None),
            P("expert", "dp", None),
        ),
        check_vma=False,
    )
```

```python
import jax
import jax.numpy as jnp
from jax import lax
from jax.experimental import pallas as pl
from jax.experimental.pallas import tpu as pltpu
from jax.sharding import PartitionSpec as P

MESH = pl.DeviceIdType.MESH
SQRT_HALF = 0.7071067811865476
INV_ROOT_TAU = 0.3989422804014327
BF = jnp.bfloat16
F32 = jnp.float32
D = 1024
FF = 2048
TOK = 256
CAP = 32
NY = 4
NZ = 4
LANES = 128


def dot(a, b, ca, cb):
    return lax.dot_general(a, b, (((ca,), (cb,)), ((), ())), preferred_element_type=F32)


def iota(shape, axis):
    return lax.broadcasted_iota(jnp.int32, shape, axis)


def to_column(row):
    n = row.shape[1]
    eye = iota((n, n), 0) == iota((n, n), 1)
    return jnp.sum(jnp.where(eye, row, 0.0), axis=1, keepdims=True)


def kernel(
    tok_hbm, og_hbm, gate_ref, id_ref, upw_hbm, dnw_hbm,
    tg_ref, gg_ref, ug_ref, dg_ref,
    tok, og, upw, dnw, slots, rows, hidden, pregrad, fgp, fgr, fgs, back,
    gown, gp, gr, ggs, ggback,
    su_out, sd_out, su_in, sd_in, zu, zd, zlu, zld, zru, zrd, fu, fd, xu, pu, pd,
    in_sem, ds_sem, dr_sem, as_sem, ar_sem, fs_sem, fr_sem, hs_sem, hr_sem,
    bs_sem, br_sem, gs_sem, gr_sem, ys_sem, yr_sem, zs_sem, zl_sem, zr_sem, xs_sem, xr_sem,
):
    dp = lax.axis_index("dp")
    ex = lax.axis_index("expert")
    y, zl = dp // NZ, dp % NZ
    zh, j = ex // 8, ex % 8
    core = ex % 2
    near = y + 1 - 2 * (y % 2)
    flip = NY - 1 - y
    yr = near + core * (flip - near)
    yf = flip + core * (near - flip)
    yd = (y + 2) % NY

    def group_dp(h):
        return y * NZ + (NZ - 1 - zl) if h else dp

    def group_ex(h, other):
        return ((1 - zh) if h else zh) * 8 + other

    def dest(h, i):
        return (group_dp(h), group_ex(h, (j + i) % 8))

    def source(h, i):
        return (group_dp(h), group_ex(h, (j + 8 - i) % 8))

    mate = (yr * NZ + zl, ex)
    twin = (yf * NZ + zl, ex)
    right = (dp + 1, ex)
    left = (dp - 1, ex)
    pairs = [(h, i) for h in (1, 0) for i in range(8) if (h, i) != (0, 0)]

    sources = [
        (tok_hbm, tok),
        (og_hbm, og),
        (upw_hbm.at[:, pl.ds(pl.multiple_of(y * 512, 512), 512)], upw.at[:, 0:512]),
        (upw_hbm.at[:, pl.ds(pl.multiple_of(yf * 512, 512), 512)], upw.at[:, 512:1024]),
        (dnw_hbm.at[pl.ds(pl.multiple_of(y * 512, 512), 512), :], dnw.at[0:512, :]),
        (dnw_hbm.at[pl.ds(pl.multiple_of(yf * 512, 512), 512), :], dnw.at[512:1024, :]),
    ]
    loads = [
        pltpu.make_async_copy(src, dst, in_sem.at[n]) for n, (src, dst) in enumerate(sources)
    ]
    for load in loads:
        load.start()

    barrier = pltpu.get_barrier_semaphore()
    for h, i in pairs:
        pl.semaphore_signal(barrier, inc=1, device_id=dest(h, i), device_id_type=MESH)
    for who in (mate, twin):
        pl.semaphore_signal(barrier, inc=1, device_id=who, device_id_type=MESH)

    @pl.when(zl < NZ - 1)
    def _():
        pl.semaphore_signal(barrier, inc=1, device_id=right, device_id_type=MESH)

    @pl.when(zl > 0)
    def _():
        pl.semaphore_signal(barrier, inc=1, device_id=left, device_id_type=MESH)

    ids = id_ref[...]
    ids_row = ids.astype(F32)
    ids_col = to_column(ids_row)
    same = ids_col == ids_row
    before = iota((TOK, TOK), 0) < iota((TOK, TOK), 1)
    after = iota((TOK, TOK), 1) < iota((TOK, TOK), 0)
    pos_row = jnp.sum(jnp.where(same & before, 1.0, 0.0), axis=0, keepdims=True)
    pos_col = jnp.sum(jnp.where(same & after, 1.0, 0.0), axis=1, keepdims=True)

    def slot_of(ident, place):
        mine = zh.astype(F32)
        half = jnp.where(ident >= 8.0, 1.0, 0.0)
        rank = ident - 8.0 * half - j.astype(F32)
        rank = jnp.where(rank < 0.0, rank + 8.0, rank)
        cross = jnp.abs(half - mine)
        return cross * 256.0 + rank * 32.0 + place

    slot_row = slot_of(ids_row, pos_row)
    slot_col = slot_of(ids_col, pos_col)
    gate_row = gate_ref[...].astype(F32).reshape(1, TOK)
    gate_col = to_column(gate_row)

    loads[0].wait()
    loads[1].wait()
    og[...] = (gate_col * og[...].astype(F32)).astype(BF)

    pl.semaphore_wait(barrier, 17 + (zl < NZ - 1).astype(jnp.int32) + (zl > 0).astype(jnp.int32))

    def dispatch(h, i):
        return pltpu.make_async_remote_copy(
            src_ref=slots.at[h, i], dst_ref=rows.at[h, i // 4, 0, i % 4],
            send_sem=ds_sem.at[h, i], recv_sem=dr_sem.at[h, i],
            device_id=dest(h, i), device_id_type=MESH,
        )

    def relay(h, i):
        src = slots.at[0, 0] if (h, i) == (0, 0) else rows.at[h, i // 4, 0, i % 4]
        return pltpu.make_async_remote_copy(
            src_ref=src, dst_ref=rows.at[h, i // 4, 1, i % 4],
            send_sem=as_sem.at[h, i], recv_sem=ar_sem.at[h, i],
            device_id=mate, device_id_type=MESH,
        )

    for h in (1, 0):
        place = (iota((TOK, TOK), 0) + TOK * h).astype(F32)
        pick = jnp.where(place == slot_row, 1.0, 0.0).astype(BF)
        slots[h, :, :CAP, :] = dot(pick, tok[...], 1, 0).astype(BF).reshape(8, CAP, D)
        slots[h, :, CAP:, :] = dot(pick, og[...], 1, 0).astype(BF).reshape(8, CAP, D)
        for i in range(8):
            if (h, i) != (0, 0):
                dispatch(h, i).start()
    relay(0, 0).start()
    rows[0, 0, 0, 0] = slots[0, 0]
    for load in loads[2:]:
        load.wait()

    def rows_of(who, h, q):
        return pl.ds((h * 2 + q) * 256 + who * LANES, LANES)

    def forward(h, q):
        here = pl.ds((h * 2 + q) * 256, 256)

        def body(n, acc):
            cols = pl.ds(pl.multiple_of(n * 512, 512), 512)
            feat = rows[h, q, :, :, :CAP, :].reshape(256, D)
            scaled = rows[h, q, :, :, CAP:, :].reshape(256, D)
            pre = dot(feat, upw[:, cols], 1, 0)
            hgrad = dot(scaled, dnw[cols, :], 1, 1)
            cdf = 0.5 * (1.0 + lax.erf(pre * SQRT_HALF))
            hid = (pre * cdf).astype(BF)
            slope = cdf + pre * jnp.exp(-0.5 * pre * pre) * INV_ROOT_TAU
            hidden[here, cols] = hid
            pregrad[here, cols] = (hgrad * slope).astype(BF)
            return acc + jnp.sum(hid.astype(F32) * hgrad, axis=1, keepdims=True)

        total = lax.fori_loop(0, 2, body, jnp.zeros((256, 1), F32))
        eye = iota((CAP, LANES), 0) == iota((CAP, LANES), 1)
        for who, out in ((0, gown), (1, gp)):
            for i in range(4):
                part = total[who * LANES + i * CAP : who * LANES + (i + 1) * CAP, :]
                row = jnp.sum(jnp.where(eye, part, 0.0), axis=0, keepdims=True)
                out[h, 4 * q + i] = jnp.broadcast_to(row, (8, LANES))

    def share_fg(h, q):
        return pltpu.make_async_remote_copy(
            src_ref=fgp.at[h, 4 * q : 4 * q + 4], dst_ref=fgr.at[h, 4 * q : 4 * q + 4],
            send_sem=fs_sem.at[h, q], recv_sem=fr_sem.at[h, q],
            device_id=mate, device_id_type=MESH,
        )

    def share_gate(h, q):
        return pltpu.make_async_remote_copy(
            src_ref=gp.at[h, 4 * q : 4 * q + 4], dst_ref=gr.at[h, 4 * q : 4 * q + 4],
            send_sem=hs_sem.at[h, q], recv_sem=hr_sem.at[h, q],
            device_id=mate, device_id_type=MESH,
        )

    def give_back(h, i):
        return pltpu.make_async_remote_copy(
            src_ref=fgs.at[h, i], dst_ref=back.at[h, i],
            send_sem=bs_sem.at[h, i], recv_sem=br_sem.at[h, i],
            device_id=source(h, i), device_id_type=MESH,
        )

    def give_gate(h, i):
        return pltpu.make_async_remote_copy(
            src_ref=ggs.at[h, i], dst_ref=ggback.at[h, i],
            send_sem=gs_sem.at[h, i], recv_sem=gr_sem.at[h, i],
            device_id=source(h, i), device_id_type=MESH,
        )

    def feature_part(who, h, q, emit):
        here = rows_of(who, h, q)

        @pl.loop(0, D // 512)
        def _(n):
            cols = pl.ds(pl.multiple_of(n * 512, 512), 512)
            emit(cols, dot(pregrad[here, :], upw[cols, :], 1, 1).reshape(4, CAP, 512))

    def mate_part(h, q):
        def emit(cols, v):
            fgp[h, 4 * q : 4 * q + 4, :, cols] = v.astype(BF)

        feature_part(1, h, q, emit)
        share_fg(h, q).start()
        share_gate(h, q).start()

    def finish(h, q):
        some = slice(4 * q, 4 * q + 4)
        share_fg(h, q).wait_recv()
        share_gate(h, q).wait_recv()

        def emit(cols, v):
            fgs[h, some, :, cols] = (v + fgr[h, some, :, cols].astype(F32)).astype(BF)

        feature_part(0, h, q, emit)
        ggs[h, some] = gown[h, some] + gr[h, some]
        for i in range(4 * q, 4 * q + 4):
            if (h, i) == (0, 0):
                back[0, 0] = fgs[0, 0]
                ggback[0, 0] = ggs[0, 0]
            else:
                give_back(h, i).start()
                give_gate(h, i).start()

    last = None
    for h, q in ((0, 0), (0, 1), (1, 0), (1, 1)):
        for i in range(4 * q, 4 * q + 4):
            if (h, i) != (0, 0):
                dispatch(h, i).wait_recv()
                relay(h, i).start()
        if last is not None:
            finish(*last)
        for i in range(4 * q, 4 * q + 4):
            relay(h, i).wait_recv()
        forward(h, q)
        mate_part(h, q)
        last = (h, q)

    def up_part(first, second, emit):
        @pl.loop(0, 2)
        def _(c):
            chunk = first + c * (second - first)
            feats = pl.ds(pl.multiple_of(chunk * 256, 256), 256)
            lhs = rows[:, :, :, :, :CAP, feats].reshape(1024, 256).T
            for n in range(2):
                emit(c, n, dot(lhs, pregrad[:, n * 512 : n * 512 + 512], 1, 0))

    def down_part(half, emit):
        @pl.loop(0, 2)
        def _(m):
            feats = pl.ds(pl.multiple_of(half * 512 + m * 256, 256), 256)
            lhs = hidden[:, feats].T
            for n in range(2):
                rhs = rows[:, :, :, :, CAP:, n * 512 : n * 512 + 512].reshape(1024, 512)
                emit(m, n, dot(lhs, rhs, 1, 0))

    def ysend(t, k):
        src, dst = ((su_out, su_in), (sd_out, sd_in))[t]
        return pltpu.make_async_remote_copy(
            src_ref=src.at[k], dst_ref=dst.at[k],
            send_sem=ys_sem.at[t, k], recv_sem=yr_sem.at[t, k],
            device_id=twin, device_id_type=MESH,
        )

    low = 1 - zl // 2

    def block(n):
        k = n // 2 + (n % 2) * (3 - 2 * (n // 2))
        return k + low * (3 - 2 * k)

    def emit_up_out(c, n, v):
        for k in range(4):
            su_out[k, c, :, (1 - n) * 512 : (2 - n) * 512] = v[64 * k : 64 * k + 64].astype(BF)

    def emit_up_own(c, n, v):
        for k in range(4):
            pu[k, c, :, n * 512 : n * 512 + 512] = v[64 * k : 64 * k + 64]

    def emit_down_out(m, n, v):
        for s in range(2):
            sd_out[2 * m + s, :, n * 512 : n * 512 + 512] = v[128 * s : 128 * s + 128].astype(BF)

    def emit_down_own(m, n, v):
        for s in range(2):
            pd[2 * m + s, :, n * 512 : n * 512 + 512] = v[128 * s : 128 * s + 128]

    zrefs = ((zu, zlu, zru), (zd, zld, zrd))

    def zright(t, k):
        src, dst, _ = zrefs[t]
        return pltpu.make_async_remote_copy(
            src_ref=src.at[k], dst_ref=dst.at[k],
            send_sem=zs_sem.at[t, k], recv_sem=zl_sem.at[t, k],
            device_id=right, device_id_type=MESH,
        )

    def zleft(t, k):
        src, _, dst = zrefs[t]
        return pltpu.make_async_remote_copy(
            src_ref=src.at[k], dst_ref=dst.at[k],
            send_sem=zs_sem.at[t, k], recv_sem=zr_sem.at[t, k],
            device_id=left, device_id_type=MESH,
        )

    def line(t, k, total, final):
        out, from_left, from_right = zrefs[t]

        @pl.when(zl == k)
        def _():
            final[...] = total[...]

        @pl.when((zl < k) & (zl == 0))
        def _():
            out[k] = total[...].astype(BF)

        @pl.when((zl < k) & (zl > 0))
        def _():
            zright(t, k).wait_recv()
            out[k] = (total[...] + from_left[k].astype(F32)).astype(BF)

        @pl.when(zl < k)
        def _():
            zright(t, k).start()

        @pl.when((zl > k) & (zl == NZ - 1))
        def _():
            out[k] = total[...].astype(BF)

        @pl.when((zl > k) & (zl < NZ - 1))
        def _():
            zleft(t, k).wait_recv()
            out[k] = (total[...] + from_right[k].astype(F32)).astype(BF)

        @pl.when(zl > k)
        def _():
            zleft(t, k).start()

    def step(t, n):
        k = block(n)
        own, came = ((pu, su_in), (pd, sd_in))[t]
        ysend(t, k).wait_recv()
        own[k] = own[k] + came[k].astype(F32)
        line(t, k, own.at[k], (fu, fd)[t])

    edge = (zl == 0) | (zl == NZ - 1)

    up_part(yf, yd, emit_up_out)
    for n in range(4):
        ysend(0, block(n)).start()
    up_part(y, yr, emit_up_own)

    @pl.when(edge)
    def _():
        step(0, 0)

    finish(*last)
    down_part(1, emit_down_out)
    for n in range(4):
        ysend(1, block(n)).start()

    @pl.when(jnp.logical_not(edge))
    def _():
        step(0, 0)

    down_part(0, emit_down_own)

    @pl.loop(1, 4)
    def _(n):
        step(0, n)

    def settle(t, final):
        _, from_left, from_right = zrefs[t]

        @pl.when(zl > 0)
        def _():
            zright(t, zl).wait_recv()
            final[...] = final[...] + from_left[zl].astype(F32)

        @pl.when(zl < NZ - 1)
        def _():
            zleft(t, zl).wait_recv()
            final[...] = final[...] + from_right[zl].astype(F32)

    for n in range(2):
        step(1, n)
    settle(0, fu)
    swap = pltpu.make_async_remote_copy(
        src_ref=fu.at[1], dst_ref=xu,
        send_sem=xs_sem.at[0], recv_sem=xr_sem.at[0],
        device_id=mate, device_id_type=MESH,
    )
    swap.start()
    for n in range(2, 4):
        step(1, n)

    for h, i in pairs:
        give_back(h, i).wait_recv()
        give_gate(h, i).wait_recv()
    spread = jnp.where(iota((TOK, 512), 1).astype(F32) == slot_col, 1.0, 0.0).astype(BF)

    @pl.loop(0, D // 512)
    def _(n):
        cols = pl.ds(pl.multiple_of(n * 512, 512), 512)
        tg_ref[:, cols] = dot(spread, back[:, :, :, cols].reshape(512, 512), 1, 0).astype(BF)

    lane = iota((TOK, LANES), 1).astype(F32)
    gate_sum = jnp.zeros((TOK, LANES), F32)
    for h in range(2):
        for i in range(8):
            base = float(h * 256 + i * CAP)
            hit = (lane < float(CAP)) & (lane + base == slot_col)
            gate_sum += jnp.where(hit, ggback[h, i, 0:1, :], 0.0)
    gate_total = jnp.sum(gate_sum, axis=1, keepdims=True) / gate_col
    eye = iota((TOK, TOK), 0) == iota((TOK, TOK), 1)
    gg_ref[...] = jnp.sum(jnp.where(eye, gate_total, 0.0), axis=0, keepdims=True).astype(BF)

    scale = 1.0 / (NY * NZ)

    def ff_chunk(c):
        return pl.ds(pl.multiple_of(c * 512, 512), 512)

    swap.wait_recv()
    ug_ref[:, ff_chunk(y)] = fu[0, :, 0:512] * scale
    ug_ref[:, ff_chunk(yf)] = fu[0, :, 512:1024] * scale
    ug_ref[:, ff_chunk(yr)] = xu[:, 0:512] * scale
    ug_ref[:, ff_chunk(yd)] = xu[:, 512:1024] * scale
    settle(1, fd)
    dg_ref[...] = fd[...] * scale

    swap.wait_send()
    relay(0, 0).wait_send()
    for h, i in pairs:
        dispatch(h, i).wait_send()
        relay(h, i).wait_send()
        give_back(h, i).wait_send()
        give_gate(h, i).wait_send()
    for h in range(2):
        for q in range(2):
            share_fg(h, q).wait_send()
            share_gate(h, q).wait_send()

    @pl.loop(0, 4)
    def _(k):
        ysend(0, k).wait_send()
        ysend(1, k).wait_send()

        @pl.when(zl != k)
        def _():
            zright(0, k).wait_send()
            zright(1, k).wait_send()


def tail(tg_in, gg_in, ug_in, dg_in, tg_out, gg_out, ug_out, dg_out, sem):
    moves = ((tg_in, tg_out), (ug_in, ug_out), (dg_in, dg_out))
    copies = [pltpu.make_async_copy(a, b, sem.at[n]) for n, (a, b) in enumerate(moves)]
    for copy in copies:
        copy.start()
    gg_out[...] = gg_in[...].reshape(TOK)
    for copy in copies:
        copy.wait()


def per_device(tokens, out_grad, gate_prob, expert_id, up_weight, down_weight):
    any_spec = pl.BlockSpec(memory_space=pl.ANY)
    vmem = pl.BlockSpec(memory_space=pltpu.VMEM)
    up_blocks = pltpu.VMEM((4, 2, 64, 1024), BF)
    down_blocks = pltpu.VMEM((4, 128, D), BF)
    grads = pltpu.VMEM((2, 8, CAP, D), BF)
    gates = pltpu.VMEM((2, 8, 8, LANES), F32)
    dma = pltpu.SemaphoreType.DMA
    tg, gg, ug, dg = pl.pallas_call(
        kernel,
        out_shape=(
            jax.ShapeDtypeStruct((TOK, D), BF),
            jax.ShapeDtypeStruct((1, TOK), BF),
            jax.ShapeDtypeStruct((64, FF), F32),
            jax.ShapeDtypeStruct((128, D), F32),
        ),
        in_specs=[any_spec, any_spec, vmem, vmem, any_spec, any_spec],
        out_specs=(vmem, vmem, vmem, vmem),
        scratch_shapes=[
            pltpu.VMEM((TOK, D), BF),
            pltpu.VMEM((TOK, D), BF),
            pltpu.VMEM((D, 1024), BF),
            pltpu.VMEM((1024, D), BF),
            pltpu.VMEM((2, 8, 2 * CAP, D), BF),
            pltpu.VMEM((2, 2, 2, 4, 2 * CAP, D), BF),
            pltpu.VMEM((1024, 1024), BF),
            pltpu.VMEM((1024, 1024), BF),
            grads, grads, grads, grads,
            gates, gates, gates, gates, gates,
            up_blocks, down_blocks, up_blocks, down_blocks, up_blocks, down_blocks,
            up_blocks, down_blocks, up_blocks, down_blocks,
            pltpu.VMEM((2, 64, 1024), F32),
            pltpu.VMEM((128, D), F32),
            pltpu.VMEM((64, 1024), F32),
            pltpu.VMEM((4, 2, 64, 1024), F32),
            pltpu.VMEM((4, 128, D), F32),
            dma((6,)),
            dma((2, 8)), dma((2, 8)), dma((2, 8)), dma((2, 8)),
            dma((2, 2)), dma((2, 2)), dma((2, 2)), dma((2, 2)),
            dma((2, 8)), dma((2, 8)), dma((2, 8)), dma((2, 8)),
            dma((2, 4)), dma((2, 4)), dma((2, 4)), dma((2, 4)), dma((2, 4)), dma((1,)), dma((1,)),
        ],
        compiler_params=pltpu.CompilerParams(
            collective_id=0, has_side_effects=True, vmem_limit_bytes=50 * 1024 * 1024
        ),
    )(
        tokens,
        out_grad,
        gate_prob,
        expert_id.reshape(1, TOK),
        up_weight[0],
        down_weight[0],
    )
    tg, gg, ug, dg = pl.pallas_call(
        tail,
        out_shape=(
            jax.ShapeDtypeStruct((TOK, D), BF),
            jax.ShapeDtypeStruct((TOK,), BF),
            jax.ShapeDtypeStruct((64, FF), F32),
            jax.ShapeDtypeStruct((128, D), F32),
        ),
        in_specs=[vmem, vmem, vmem, vmem],
        out_specs=(any_spec, vmem, any_spec, any_spec),
        scratch_shapes=[
            dma((3,)),
        ],
        compiler_params=pltpu.CompilerParams(vmem_limit_bytes=2 * 1024 * 1024),
    )(tg, gg, ug, dg)
    return tg, gg, ug[None], dg[None]


def solution(mesh):
    return jax.shard_map(
        per_device,
        mesh=mesh,
        in_specs=(
            P(("dp", "expert"), None),
            P(("dp", "expert"), None),
            P(("dp", "expert")),
            P(("dp", "expert")),
            P("expert", None, None),
            P("expert", None, None),
        ),
        out_specs=(
            P(("dp", "expert"), None),
            P(("dp", "expert")),
            P("expert", "dp", None),
            P("expert", "dp", None),
        ),
        check_vma=False,
    )
```

```python
import jax
import jax.numpy as jnp
from jax import lax
from jax.experimental import pallas as pl
from jax.experimental.pallas import tpu as pltpu
from jax.sharding import PartitionSpec as P

MESH = pl.DeviceIdType.MESH
SQRT_HALF = 0.7071067811865476
INV_ROOT_TAU = 0.3989422804014327
BF = jnp.bfloat16
F32 = jnp.float32
D = 1024
FF = 2048
TOK = 256
CAP = 32
NY = 4
NZ = 4
LANES = 128


def dot(a, b, ca, cb):
    return lax.dot_general(a, b, (((ca,), (cb,)), ((), ())), preferred_element_type=F32)


def iota(shape, axis):
    return lax.broadcasted_iota(jnp.int32, shape, axis)


def to_column(row):
    n = row.shape[1]
    eye = iota((n, n), 0) == iota((n, n), 1)
    return jnp.sum(jnp.where(eye, row, 0.0), axis=1, keepdims=True)


def kernel(
    tok_hbm, og_hbm, gate_hbm, id_hbm, upw_hbm, dnw_hbm,
    tg_ref, gg_ref, ug_ref, dg_ref,
    gate_ref, id_ref, tok, og, upw, dnw, slots, rows, hidden, pregrad, fgp, fgr, fgs, back,
    gown, gp, gr, ggs, ggback,
    su_out, sd_out, su_in, sd_in, zu, zd, zlu, zld, zru, zrd, fu, fd, xu, pu, pd,
    in_sem, ds_sem, dr_sem, as_sem, ar_sem, fs_sem, fr_sem, hs_sem, hr_sem,
    bs_sem, br_sem, gs_sem, gr_sem, ys_sem, yr_sem, zs_sem, zl_sem, zr_sem, xs_sem, xr_sem,
):
    dp = lax.axis_index("dp")
    ex = lax.axis_index("expert")
    y, zl = dp // NZ, dp % NZ
    zh, j = ex // 8, ex % 8
    core = ex % 2
    near = y + 1 - 2 * (y % 2)
    flip = NY - 1 - y
    yr = near + core * (flip - near)
    yf = flip + core * (near - flip)
    yd = (y + 2) % NY

    def group_dp(h):
        return y * NZ + (NZ - 1 - zl) if h else dp

    def group_ex(h, other):
        return ((1 - zh) if h else zh) * 8 + other

    def dest(h, i):
        return (group_dp(h), group_ex(h, (j + i) % 8))

    def source(h, i):
        return (group_dp(h), group_ex(h, (j + 8 - i) % 8))

    mate = (yr * NZ + zl, ex)
    twin = (yf * NZ + zl, ex)
    right = (dp + 1, ex)
    left = (dp - 1, ex)
    pairs = [(h, i) for h in (1, 0) for i in range(8) if (h, i) != (0, 0)]

    sources = [
        (id_hbm, id_ref),
        (gate_hbm, gate_ref),
        (tok_hbm, tok),
        (og_hbm, og),
        (upw_hbm.at[:, pl.ds(pl.multiple_of(y * 512, 512), 512)], upw.at[:, 0:512]),
        (upw_hbm.at[:, pl.ds(pl.multiple_of(yf * 512, 512), 512)], upw.at[:, 512:1024]),
        (dnw_hbm.at[pl.ds(pl.multiple_of(y * 512, 512), 512), :], dnw.at[0:512, :]),
        (dnw_hbm.at[pl.ds(pl.multiple_of(yf * 512, 512), 512), :], dnw.at[512:1024, :]),
    ]
    loads = [
        pltpu.make_async_copy(src, dst, in_sem.at[n]) for n, (src, dst) in enumerate(sources)
    ]
    for load in loads:
        load.start()

    barrier = pltpu.get_barrier_semaphore()
    for h, i in pairs:
        pl.semaphore_signal(barrier, inc=1, device_id=dest(h, i), device_id_type=MESH)
    for who in (mate, twin):
        pl.semaphore_signal(barrier, inc=1, device_id=who, device_id_type=MESH)

    @pl.when(zl < NZ - 1)
    def _():
        pl.semaphore_signal(barrier, inc=1, device_id=right, device_id_type=MESH)

    @pl.when(zl > 0)
    def _():
        pl.semaphore_signal(barrier, inc=1, device_id=left, device_id_type=MESH)

    loads[0].wait()
    loads[1].wait()
    ids = id_ref[...]
    ids_row = ids.astype(F32)
    ids_col = to_column(ids_row)
    same = ids_col == ids_row
    before = iota((TOK, TOK), 0) < iota((TOK, TOK), 1)
    after = iota((TOK, TOK), 1) < iota((TOK, TOK), 0)
    pos_row = jnp.sum(jnp.where(same & before, 1.0, 0.0), axis=0, keepdims=True)
    pos_col = jnp.sum(jnp.where(same & after, 1.0, 0.0), axis=1, keepdims=True)

    def slot_of(ident, place):
        mine = zh.astype(F32)
        half = jnp.where(ident >= 8.0, 1.0, 0.0)
        rank = ident - 8.0 * half - j.astype(F32)
        rank = jnp.where(rank < 0.0, rank + 8.0, rank)
        cross = jnp.abs(half - mine)
        return cross * 256.0 + rank * 32.0 + place

    slot_row = slot_of(ids_row, pos_row)
    slot_col = slot_of(ids_col, pos_col)
    gate_row = gate_ref[...].astype(F32).reshape(1, TOK)
    gate_col = to_column(gate_row)

    loads[2].wait()
    loads[3].wait()
    og[...] = (gate_col * og[...].astype(F32)).astype(BF)

    pl.semaphore_wait(barrier, 17 + (zl < NZ - 1).astype(jnp.int32) + (zl > 0).astype(jnp.int32))

    def dispatch(h, i):
        return pltpu.make_async_remote_copy(
            src_ref=slots.at[h, i], dst_ref=rows.at[h, i // 4, 0, i % 4],
            send_sem=ds_sem.at[h, i], recv_sem=dr_sem.at[h, i],
            device_id=dest(h, i), device_id_type=MESH,
        )

    def relay(h, i):
        src = slots.at[0, 0] if (h, i) == (0, 0) else rows.at[h, i // 4, 0, i % 4]
        return pltpu.make_async_remote_copy(
            src_ref=src, dst_ref=rows.at[h, i // 4, 1, i % 4],
            send_sem=as_sem.at[h, i], recv_sem=ar_sem.at[h, i],
            device_id=mate, device_id_type=MESH,
        )

    for h in (1, 0):
        place = (iota((TOK, TOK), 0) + TOK * h).astype(F32)
        pick = jnp.where(place == slot_row, 1.0, 0.0).astype(BF)
        slots[h, :, :CAP, :] = dot(pick, tok[...], 1, 0).astype(BF).reshape(8, CAP, D)
        slots[h, :, CAP:, :] = dot(pick, og[...], 1, 0).astype(BF).reshape(8, CAP, D)
        for i in range(8):
            if (h, i) != (0, 0):
                dispatch(h, i).start()
    relay(0, 0).start()
    rows[0, 0, 0, 0] = slots[0, 0]
    for load in loads[4:]:
        load.wait()

    def rows_of(who, h, q):
        return pl.ds((h * 2 + q) * 256 + who * LANES, LANES)

    def forward(h, q):
        here = pl.ds((h * 2 + q) * 256, 256)

        def body(n, acc):
            cols = pl.ds(pl.multiple_of(n * 512, 512), 512)
            feat = rows[h, q, :, :, :CAP, :].reshape(256, D)
            scaled = rows[h, q, :, :, CAP:, :].reshape(256, D)
            pre = dot(feat, upw[:, cols], 1, 0)
            hgrad = dot(scaled, dnw[cols, :], 1, 1)
            cdf = 0.5 * (1.0 + lax.erf(pre * SQRT_HALF))
            hid = (pre * cdf).astype(BF)
            slope = cdf + pre * jnp.exp(-0.5 * pre * pre) * INV_ROOT_TAU
            hidden[here, cols] = hid
            pregrad[here, cols] = (hgrad * slope).astype(BF)
            return acc + jnp.sum(hid.astype(F32) * hgrad, axis=1, keepdims=True)

        total = lax.fori_loop(0, 2, body, jnp.zeros((256, 1), F32))
        eye = iota((CAP, LANES), 0) == iota((CAP, LANES), 1)
        for who, out in ((0, gown), (1, gp)):
            for i in range(4):
                part = total[who * LANES + i * CAP : who * LANES + (i + 1) * CAP, :]
                row = jnp.sum(jnp.where(eye, part, 0.0), axis=0, keepdims=True)
                out[h, 4 * q + i] = jnp.broadcast_to(row, (8, LANES))

    def share_fg(h, q):
        return pltpu.make_async_remote_copy(
            src_ref=fgp.at[h, 4 * q : 4 * q + 4], dst_ref=fgr.at[h, 4 * q : 4 * q + 4],
            send_sem=fs_sem.at[h, q], recv_sem=fr_sem.at[h, q],
            device_id=mate, device_id_type=MESH,
        )

    def share_gate(h, q):
        return pltpu.make_async_remote_copy(
            src_ref=gp.at[h, 4 * q : 4 * q + 4], dst_ref=gr.at[h, 4 * q : 4 * q + 4],
            send_sem=hs_sem.at[h, q], recv_sem=hr_sem.at[h, q],
            device_id=mate, device_id_type=MESH,
        )

    def give_back(h, i):
        return pltpu.make_async_remote_copy(
            src_ref=fgs.at[h, i], dst_ref=back.at[h, i],
            send_sem=bs_sem.at[h, i], recv_sem=br_sem.at[h, i],
            device_id=source(h, i), device_id_type=MESH,
        )

    def give_gate(h, i):
        return pltpu.make_async_remote_copy(
            src_ref=ggs.at[h, i], dst_ref=ggback.at[h, i],
            send_sem=gs_sem.at[h, i], recv_sem=gr_sem.at[h, i],
            device_id=source(h, i), device_id_type=MESH,
        )

    def feature_part(who, h, q, emit):
        here = rows_of(who, h, q)

        @pl.loop(0, D // 512)
        def _(n):
            cols = pl.ds(pl.multiple_of(n * 512, 512), 512)
            emit(cols, dot(pregrad[here, :], upw[cols, :], 1, 1).reshape(4, CAP, 512))

    def mate_part(h, q):
        def emit(cols, v):
            fgp[h, 4 * q : 4 * q + 4, :, cols] = v.astype(BF)

        feature_part(1, h, q, emit)
        share_fg(h, q).start()
        share_gate(h, q).start()

    def finish(h, q):
        some = slice(4 * q, 4 * q + 4)
        share_fg(h, q).wait_recv()
        share_gate(h, q).wait_recv()

        def emit(cols, v):
            fgs[h, some, :, cols] = (v + fgr[h, some, :, cols].astype(F32)).astype(BF)

        feature_part(0, h, q, emit)
        ggs[h, some] = gown[h, some] + gr[h, some]
        for i in range(4 * q, 4 * q + 4):
            if (h, i) == (0, 0):
                back[0, 0] = fgs[0, 0]
                ggback[0, 0] = ggs[0, 0]
            else:
                give_back(h, i).start()
                give_gate(h, i).start()

    last = None
    for h, q in ((0, 0), (0, 1), (1, 0), (1, 1)):
        for i in range(4 * q, 4 * q + 4):
            if (h, i) != (0, 0):
                dispatch(h, i).wait_recv()
                relay(h, i).start()
        if last is not None:
            finish(*last)
        for i in range(4 * q, 4 * q + 4):
            relay(h, i).wait_recv()
        forward(h, q)
        mate_part(h, q)
        last = (h, q)

    def up_part(first, second, emit):
        @pl.loop(0, 2)
        def _(c):
            chunk = first + c * (second - first)
            feats = pl.ds(pl.multiple_of(chunk * 256, 256), 256)
            lhs = rows[:, :, :, :, :CAP, feats].reshape(1024, 256).T
            for n in range(2):
                emit(c, n, dot(lhs, pregrad[:, n * 512 : n * 512 + 512], 1, 0))

    def down_part(half, emit):
        @pl.loop(0, 2)
        def _(m):
            feats = pl.ds(pl.multiple_of(half * 512 + m * 256, 256), 256)
            lhs = hidden[:, feats].T
            for n in range(2):
                rhs = rows[:, :, :, :, CAP:, n * 512 : n * 512 + 512].reshape(1024, 512)
                emit(m, n, dot(lhs, rhs, 1, 0))

    def ysend(t, k):
        src, dst = ((su_out, su_in), (sd_out, sd_in))[t]
        return pltpu.make_async_remote_copy(
            src_ref=src.at[k], dst_ref=dst.at[k],
            send_sem=ys_sem.at[t, k], recv_sem=yr_sem.at[t, k],
            device_id=twin, device_id_type=MESH,
        )

    low = 1 - zl // 2

    def block(n):
        k = n // 2 + (n % 2) * (3 - 2 * (n // 2))
        return k + low * (3 - 2 * k)

    def emit_up_out(c, n, v):
        for k in range(4):
            su_out[k, c, :, (1 - n) * 512 : (2 - n) * 512] = v[64 * k : 64 * k + 64].astype(BF)

    def emit_up_own(c, n, v):
        for k in range(4):
            pu[k, c, :, n * 512 : n * 512 + 512] = v[64 * k : 64 * k + 64]

    def emit_down_out(m, n, v):
        for s in range(2):
            sd_out[2 * m + s, :, n * 512 : n * 512 + 512] = v[128 * s : 128 * s + 128].astype(BF)

    def emit_down_own(m, n, v):
        for s in range(2):
            pd[2 * m + s, :, n * 512 : n * 512 + 512] = v[128 * s : 128 * s + 128]

    zrefs = ((zu, zlu, zru), (zd, zld, zrd))

    def zright(t, k):
        src, dst, _ = zrefs[t]
        return pltpu.make_async_remote_copy(
            src_ref=src.at[k], dst_ref=dst.at[k],
            send_sem=zs_sem.at[t, k], recv_sem=zl_sem.at[t, k],
            device_id=right, device_id_type=MESH,
        )

    def zleft(t, k):
        src, _, dst = zrefs[t]
        return pltpu.make_async_remote_copy(
            src_ref=src.at[k], dst_ref=dst.at[k],
            send_sem=zs_sem.at[t, k], recv_sem=zr_sem.at[t, k],
            device_id=left, device_id_type=MESH,
        )

    def line(t, k, total, final):
        out, from_left, from_right = zrefs[t]

        @pl.when(zl == k)
        def _():
            final[...] = total[...]

        @pl.when((zl < k) & (zl == 0))
        def _():
            out[k] = total[...].astype(BF)

        @pl.when((zl < k) & (zl > 0))
        def _():
            zright(t, k).wait_recv()
            out[k] = (total[...] + from_left[k].astype(F32)).astype(BF)

        @pl.when(zl < k)
        def _():
            zright(t, k).start()

        @pl.when((zl > k) & (zl == NZ - 1))
        def _():
            out[k] = total[...].astype(BF)

        @pl.when((zl > k) & (zl < NZ - 1))
        def _():
            zleft(t, k).wait_recv()
            out[k] = (total[...] + from_right[k].astype(F32)).astype(BF)

        @pl.when(zl > k)
        def _():
            zleft(t, k).start()

    def step(t, n):
        k = block(n)
        own, came = ((pu, su_in), (pd, sd_in))[t]
        ysend(t, k).wait_recv()
        own[k] = own[k] + came[k].astype(F32)
        line(t, k, own.at[k], (fu, fd)[t])

    edge = (zl == 0) | (zl == NZ - 1)

    up_part(yf, yd, emit_up_out)
    for n in range(4):
        ysend(0, block(n)).start()
    up_part(y, yr, emit_up_own)

    @pl.when(edge)
    def _():
        step(0, 0)

    finish(*last)
    down_part(1, emit_down_out)
    for n in range(4):
        ysend(1, block(n)).start()

    @pl.when(jnp.logical_not(edge))
    def _():
        step(0, 0)

    down_part(0, emit_down_own)

    @pl.loop(1, 4)
    def _(n):
        step(0, n)

    def settle(t, final):
        _, from_left, from_right = zrefs[t]

        @pl.when(zl > 0)
        def _():
            zright(t, zl).wait_recv()
            final[...] = final[...] + from_left[zl].astype(F32)

        @pl.when(zl < NZ - 1)
        def _():
            zleft(t, zl).wait_recv()
            final[...] = final[...] + from_right[zl].astype(F32)

    for n in range(2):
        step(1, n)
    settle(0, fu)
    swap = pltpu.make_async_remote_copy(
        src_ref=fu.at[1], dst_ref=xu,
        send_sem=xs_sem.at[0], recv_sem=xr_sem.at[0],
        device_id=mate, device_id_type=MESH,
    )
    swap.start()
    for n in range(2, 4):
        step(1, n)

    for h, i in pairs:
        give_back(h, i).wait_recv()
        give_gate(h, i).wait_recv()
    spread = jnp.where(iota((TOK, 512), 1).astype(F32) == slot_col, 1.0, 0.0).astype(BF)

    @pl.loop(0, D // 512)
    def _(n):
        cols = pl.ds(pl.multiple_of(n * 512, 512), 512)
        tg_ref[:, cols] = dot(spread, back[:, :, :, cols].reshape(512, 512), 1, 0).astype(BF)

    lane = iota((TOK, LANES), 1).astype(F32)
    gate_sum = jnp.zeros((TOK, LANES), F32)
    for h in range(2):
        for i in range(8):
            base = float(h * 256 + i * CAP)
            hit = (lane < float(CAP)) & (lane + base == slot_col)
            gate_sum += jnp.where(hit, ggback[h, i, 0:1, :], 0.0)
    gate_total = jnp.sum(gate_sum, axis=1, keepdims=True) / gate_col
    eye = iota((TOK, TOK), 0) == iota((TOK, TOK), 1)
    gg_ref[...] = jnp.sum(jnp.where(eye, gate_total, 0.0), axis=0, keepdims=True).astype(BF)

    scale = 1.0 / (NY * NZ)

    def ff_chunk(c):
        return pl.ds(pl.multiple_of(c * 512, 512), 512)

    swap.wait_recv()
    ug_ref[:, ff_chunk(y)] = fu[0, :, 0:512] * scale
    ug_ref[:, ff_chunk(yf)] = fu[0, :, 512:1024] * scale
    ug_ref[:, ff_chunk(yr)] = xu[:, 0:512] * scale
    ug_ref[:, ff_chunk(yd)] = xu[:, 512:1024] * scale
    settle(1, fd)
    dg_ref[...] = fd[...] * scale

    swap.wait_send()
    relay(0, 0).wait_send()
    for h, i in pairs:
        dispatch(h, i).wait_send()
        relay(h, i).wait_send()
        give_back(h, i).wait_send()
        give_gate(h, i).wait_send()
    for h in range(2):
        for q in range(2):
            share_fg(h, q).wait_send()
            share_gate(h, q).wait_send()

    @pl.loop(0, 4)
    def _(k):
        ysend(0, k).wait_send()
        ysend(1, k).wait_send()

        @pl.when(zl != k)
        def _():
            zright(0, k).wait_send()
            zright(1, k).wait_send()


def tail(tg_in, gg_in, ug_in, dg_in, tg_out, gg_out, ug_out, dg_out, sem):
    moves = ((tg_in, tg_out), (ug_in, ug_out), (dg_in, dg_out))
    copies = [pltpu.make_async_copy(a, b, sem.at[n]) for n, (a, b) in enumerate(moves)]
    for copy in copies:
        copy.start()
    gg_out[...] = gg_in[...].reshape(TOK)
    for copy in copies:
        copy.wait()


def per_device(tokens, out_grad, gate_prob, expert_id, up_weight, down_weight):
    any_spec = pl.BlockSpec(memory_space=pl.ANY)
    vmem = pl.BlockSpec(memory_space=pltpu.VMEM)
    up_blocks = pltpu.VMEM((4, 2, 64, 1024), BF)
    down_blocks = pltpu.VMEM((4, 128, D), BF)
    grads = pltpu.VMEM((2, 8, CAP, D), BF)
    gates = pltpu.VMEM((2, 8, 8, LANES), F32)
    dma = pltpu.SemaphoreType.DMA
    tg, gg, ug, dg = pl.pallas_call(
        kernel,
        out_shape=(
            jax.ShapeDtypeStruct((TOK, D), BF),
            jax.ShapeDtypeStruct((1, TOK), BF),
            jax.ShapeDtypeStruct((64, FF), F32),
            jax.ShapeDtypeStruct((128, D), F32),
        ),
        in_specs=[any_spec] * 6,
        out_specs=(vmem, vmem, vmem, vmem),
        scratch_shapes=[
            pltpu.VMEM((TOK,), BF),
            pltpu.VMEM((1, TOK), jnp.int32),
            pltpu.VMEM((TOK, D), BF),
            pltpu.VMEM((TOK, D), BF),
            pltpu.VMEM((D, 1024), BF),
            pltpu.VMEM((1024, D), BF),
            pltpu.VMEM((2, 8, 2 * CAP, D), BF),
            pltpu.VMEM((2, 2, 2, 4, 2 * CAP, D), BF),
            pltpu.VMEM((1024, 1024), BF),
            pltpu.VMEM((1024, 1024), BF),
            grads, grads, grads, grads,
            gates, gates, gates, gates, gates,
            up_blocks, down_blocks, up_blocks, down_blocks, up_blocks, down_blocks,
            up_blocks, down_blocks, up_blocks, down_blocks,
            pltpu.VMEM((2, 64, 1024), F32),
            pltpu.VMEM((128, D), F32),
            pltpu.VMEM((64, 1024), F32),
            pltpu.VMEM((4, 2, 64, 1024), F32),
            pltpu.VMEM((4, 128, D), F32),
            dma((8,)),
            dma((2, 8)), dma((2, 8)), dma((2, 8)), dma((2, 8)),
            dma((2, 2)), dma((2, 2)), dma((2, 2)), dma((2, 2)),
            dma((2, 8)), dma((2, 8)), dma((2, 8)), dma((2, 8)),
            dma((2, 4)), dma((2, 4)), dma((2, 4)), dma((2, 4)), dma((2, 4)), dma((1,)), dma((1,)),
        ],
        compiler_params=pltpu.CompilerParams(
            collective_id=0, has_side_effects=True, vmem_limit_bytes=52 * 1024 * 1024
        ),
    )(
        *(
            pltpu.with_memory_space_constraint(x, pltpu.HBM)
            for x in (tokens, out_grad, gate_prob, expert_id.reshape(1, TOK))
        ),
        up_weight[0],
        down_weight[0],
    )
    tg, gg, ug, dg = pl.pallas_call(
        tail,
        out_shape=(
            jax.ShapeDtypeStruct((TOK, D), BF),
            jax.ShapeDtypeStruct((TOK,), BF),
            jax.ShapeDtypeStruct((64, FF), F32),
            jax.ShapeDtypeStruct((128, D), F32),
        ),
        in_specs=[vmem, vmem, vmem, vmem],
        out_specs=(any_spec, vmem, any_spec, any_spec),
        scratch_shapes=[
            dma((3,)),
        ],
        compiler_params=pltpu.CompilerParams(vmem_limit_bytes=2 * 1024 * 1024),
    )(tg, gg, ug, dg)
    return tg, gg, ug[None], dg[None]


def solution(mesh):
    return jax.shard_map(
        per_device,
        mesh=mesh,
        in_specs=(
            P(("dp", "expert"), None),
            P(("dp", "expert"), None),
            P(("dp", "expert")),
            P(("dp", "expert")),
            P("expert", None, None),
            P("expert", None, None),
        ),
        out_specs=(
            P(("dp", "expert"), None),
            P(("dp", "expert")),
            P("expert", "dp", None),
            P("expert", "dp", None),
        ),
        check_vma=False,
    )
```

```python
import jax
import jax.numpy as jnp
from jax import lax
from jax.experimental import pallas as pl
from jax.experimental.pallas import tpu as pltpu
from jax.sharding import PartitionSpec as P

MESH = pl.DeviceIdType.MESH
SQRT_HALF = 0.7071067811865476
INV_ROOT_TAU = 0.3989422804014327
BF = jnp.bfloat16
F32 = jnp.float32
D = 1024
FF = 2048
TOK = 256
CAP = 32
NY = 4
NZ = 4
LANES = 128
AWAY = (0, 1, 2, 3, 6, 7, 4, 5)


def dot(a, b, ca, cb):
    return lax.dot_general(a, b, (((ca,), (cb,)), ((), ())), preferred_element_type=F32)


def iota(shape, axis):
    return lax.broadcasted_iota(jnp.int32, shape, axis)


def to_column(row):
    n = row.shape[1]
    eye = iota((n, n), 0) == iota((n, n), 1)
    return jnp.sum(jnp.where(eye, row, 0.0), axis=1, keepdims=True)


def kernel(
    tok_hbm, og_hbm, gate_hbm, id_hbm, upw_hbm, dnw_hbm,
    tg_ref, gg_ref, ug_ref, dg_ref,
    gate_ref, id_ref, tok, og, upw, dnw, slots, rows, hidden, pregrad, fgp, fgr, fgs, back,
    gown, gp, gr, ggs, ggback,
    su_out, sd_out, su_in, sd_in, zu, zd, zlu, zld, zru, zrd, fu, fd, xu, pu, pd,
    in_sem, ds_sem, dr_sem, as_sem, ar_sem, fs_sem, fr_sem, hs_sem, hr_sem,
    bs_sem, br_sem, gs_sem, gr_sem, ys_sem, yr_sem, zs_sem, zl_sem, zr_sem, xs_sem, xr_sem,
):
    dp = lax.axis_index("dp")
    ex = lax.axis_index("expert")
    y, zl = dp // NZ, dp % NZ
    zh, j = ex // 8, ex % 8
    core = ex % 2
    near = y + 1 - 2 * (y % 2)
    flip = NY - 1 - y
    yr = near + core * (flip - near)
    yf = flip + core * (near - flip)
    yd = (y + 2) % NY

    def group_dp(h):
        return y * NZ + (NZ - 1 - zl) if h else dp

    def group_ex(h, other):
        return ((1 - zh) if h else zh) * 8 + other

    def dest(h, i):
        return (group_dp(h), group_ex(h, (j + AWAY[i]) % 8))

    def source(h, i):
        return (group_dp(h), group_ex(h, (j + 8 - AWAY[i]) % 8))

    mate = (yr * NZ + zl, ex)
    twin = (yf * NZ + zl, ex)
    right = (dp + 1, ex)
    left = (dp - 1, ex)
    pairs = [(h, i) for h in (1, 0) for i in range(8) if (h, i) != (0, 0)]

    sources = [
        (id_hbm, id_ref),
        (gate_hbm, gate_ref),
        (tok_hbm, tok),
        (og_hbm, og),
        (upw_hbm.at[:, pl.ds(pl.multiple_of(y * 512, 512), 512)], upw.at[:, 0:512]),
        (upw_hbm.at[:, pl.ds(pl.multiple_of(yf * 512, 512), 512)], upw.at[:, 512:1024]),
        (dnw_hbm.at[pl.ds(pl.multiple_of(y * 512, 512), 512), :], dnw.at[0:512, :]),
        (dnw_hbm.at[pl.ds(pl.multiple_of(yf * 512, 512), 512), :], dnw.at[512:1024, :]),
    ]
    loads = [
        pltpu.make_async_copy(src, dst, in_sem.at[n]) for n, (src, dst) in enumerate(sources)
    ]
    for load in loads:
        load.start()

    barrier = pltpu.get_barrier_semaphore()
    for h, i in pairs:
        pl.semaphore_signal(barrier, inc=1, device_id=dest(h, i), device_id_type=MESH)
    for who in (mate, twin):
        pl.semaphore_signal(barrier, inc=1, device_id=who, device_id_type=MESH)

    @pl.when(zl < NZ - 1)
    def _():
        pl.semaphore_signal(barrier, inc=1, device_id=right, device_id_type=MESH)

    @pl.when(zl > 0)
    def _():
        pl.semaphore_signal(barrier, inc=1, device_id=left, device_id_type=MESH)

    loads[0].wait()
    loads[1].wait()
    ids = id_ref[...]
    ids_row = ids.astype(F32)
    ids_col = to_column(ids_row)
    same = ids_col == ids_row
    before = iota((TOK, TOK), 0) < iota((TOK, TOK), 1)
    after = iota((TOK, TOK), 1) < iota((TOK, TOK), 0)
    pos_row = jnp.sum(jnp.where(same & before, 1.0, 0.0), axis=0, keepdims=True)
    pos_col = jnp.sum(jnp.where(same & after, 1.0, 0.0), axis=1, keepdims=True)

    def slot_of(ident, place):
        mine = zh.astype(F32)
        half = jnp.where(ident >= 8.0, 1.0, 0.0)
        rank = ident - 8.0 * half - j.astype(F32)
        rank = jnp.where(rank < 0.0, rank + 8.0, rank)
        rank = rank + jnp.where(rank >= 6.0, -2.0, jnp.where(rank >= 4.0, 2.0, 0.0))
        cross = jnp.abs(half - mine)
        return cross * 256.0 + rank * 32.0 + place

    slot_row = slot_of(ids_row, pos_row)
    slot_col = slot_of(ids_col, pos_col)
    gate_row = gate_ref[...].astype(F32).reshape(1, TOK)
    gate_col = to_column(gate_row)

    loads[2].wait()
    loads[3].wait()
    og[...] = (gate_col * og[...].astype(F32)).astype(BF)

    pl.semaphore_wait(barrier, 17 + (zl < NZ - 1).astype(jnp.int32) + (zl > 0).astype(jnp.int32))

    def dispatch(h, i):
        return pltpu.make_async_remote_copy(
            src_ref=slots.at[h, i], dst_ref=rows.at[h, i // 2, 0, i % 2],
            send_sem=ds_sem.at[h, i], recv_sem=dr_sem.at[h, i],
            device_id=dest(h, i), device_id_type=MESH,
        )

    def relay(h, i):
        src = slots.at[0, 0] if (h, i) == (0, 0) else rows.at[h, i // 2, 0, i % 2]
        return pltpu.make_async_remote_copy(
            src_ref=src, dst_ref=rows.at[h, i // 2, 1, i % 2],
            send_sem=as_sem.at[h, i], recv_sem=ar_sem.at[h, i],
            device_id=mate, device_id_type=MESH,
        )

    for h in (1, 0):
        place = (iota((TOK, TOK), 0) + TOK * h).astype(F32)
        pick = jnp.where(place == slot_row, 1.0, 0.0).astype(BF)
        slots[h, :, :CAP, :] = dot(pick, tok[...], 1, 0).astype(BF).reshape(8, CAP, D)
        slots[h, :, CAP:, :] = dot(pick, og[...], 1, 0).astype(BF).reshape(8, CAP, D)
        for i in range(8):
            if (h, i) != (0, 0):
                dispatch(h, i).start()
    relay(0, 0).start()
    rows[0, 0, 0, 0] = slots[0, 0]
    for load in loads[4:]:
        load.wait()

    def forward(h, first, count):
        size = count * 2 * CAP
        here = pl.ds((h * 8 + first) * 2 * CAP, size)
        some = slice(first // 2, (first + count) // 2)
        total = jnp.zeros((size, 1), F32)
        for n in range(2):
            cols = slice(n * 512, n * 512 + 512)
            feat = rows[h, some, :, :, :CAP, :].reshape(size, D)
            scaled = rows[h, some, :, :, CAP:, :].reshape(size, D)
            pre = dot(feat, upw[:, cols], 1, 0)
            hgrad = dot(scaled, dnw[cols, :], 1, 1)
            cdf = 0.5 * (1.0 + lax.erf(pre * SQRT_HALF))
            hid = (pre * cdf).astype(BF)
            slope = cdf + pre * jnp.exp(-0.5 * pre * pre) * INV_ROOT_TAU
            hidden[here, cols] = hid
            pregrad[here, cols] = (hgrad * slope).astype(BF)
            total += jnp.sum(hid.astype(F32) * hgrad, axis=1, keepdims=True)
        eye = iota((CAP, LANES), 0) == iota((CAP, LANES), 1)
        for pair in range(count // 2):
            for who, out in ((0, gown), (1, gp)):
                for i in range(2):
                    start = (pair * 4 + who * 2 + i) * CAP
                    part = total[start : start + CAP, :]
                    row = jnp.sum(jnp.where(eye, part, 0.0), axis=0, keepdims=True)
                    out[h, first + 2 * pair + i] = jnp.broadcast_to(row, (8, LANES))

    def share_fg(h, q):
        return pltpu.make_async_remote_copy(
            src_ref=fgp.at[h, 4 * q : 4 * q + 4], dst_ref=fgr.at[h, 4 * q : 4 * q + 4],
            send_sem=fs_sem.at[h, q], recv_sem=fr_sem.at[h, q],
            device_id=mate, device_id_type=MESH,
        )

    def share_gate(h, q):
        return pltpu.make_async_remote_copy(
            src_ref=gp.at[h, 4 * q : 4 * q + 4], dst_ref=gr.at[h, 4 * q : 4 * q + 4],
            send_sem=hs_sem.at[h, q], recv_sem=hr_sem.at[h, q],
            device_id=mate, device_id_type=MESH,
        )

    def give_back(h, i):
        return pltpu.make_async_remote_copy(
            src_ref=fgs.at[h, i], dst_ref=back.at[h, i],
            send_sem=bs_sem.at[h, i], recv_sem=br_sem.at[h, i],
            device_id=source(h, i), device_id_type=MESH,
        )

    def give_gate(h, i):
        return pltpu.make_async_remote_copy(
            src_ref=ggs.at[h, i], dst_ref=ggback.at[h, i],
            send_sem=gs_sem.at[h, i], recv_sem=gr_sem.at[h, i],
            device_id=source(h, i), device_id_type=MESH,
        )

    def feature_part(who, h, q, emit):
        @pl.loop(0, D // 512)
        def _(n):
            cols = pl.ds(pl.multiple_of(n * 512, 512), 512)
            base = (h * 8 + 4 * q) * 2 * CAP + who * 2 * CAP
            lhs = jnp.concatenate(
                [pregrad[pl.ds(base + p * 4 * CAP, 2 * CAP), :] for p in range(2)], axis=0
            )
            emit(cols, dot(lhs, upw[cols, :], 1, 1).reshape(4, CAP, 512))

    def mate_part(h, q):
        def emit(cols, v):
            fgp[h, 4 * q : 4 * q + 4, :, cols] = v.astype(BF)

        feature_part(1, h, q, emit)
        share_fg(h, q).start()
        share_gate(h, q).start()

    def finish(h, q):
        some = slice(4 * q, 4 * q + 4)
        share_fg(h, q).wait_recv()
        share_gate(h, q).wait_recv()

        def emit(cols, v):
            fgs[h, some, :, cols] = (v + fgr[h, some, :, cols].astype(F32)).astype(BF)

        feature_part(0, h, q, emit)
        ggs[h, some] = gown[h, some] + gr[h, some]
        for i in range(4 * q, 4 * q + 4):
            if (h, i) == (0, 0):
                back[0, 0] = fgs[0, 0]
                ggback[0, 0] = ggs[0, 0]
            else:
                give_back(h, i).start()
                give_gate(h, i).start()

    last = None
    for h, q in ((0, 0), (0, 1), (1, 0), (1, 1)):
        final = (h, q) == (1, 1)
        for first, count in ((4 * q, 2), (4 * q + 2, 2)) if final else ((4 * q, 4),):
            for i in range(first, first + count):
                if (h, i) != (0, 0):
                    dispatch(h, i).wait_recv()
                    relay(h, i).start()
            if last is not None and first == 4 * q:
                finish(*last)
            for i in range(first, first + count):
                relay(h, i).wait_recv()
            forward(h, first, count)
        mate_part(h, q)
        last = (h, q)

    low = 1 - zl // 2

    def block(n):
        k = n // 2 + (n % 2) * (3 - 2 * (n // 2))
        return k + low * (3 - 2 * k)

    def up_part(first, second, emit):
        @pl.loop(0, 2)
        def _(c):
            chunk = first + c * (second - first)
            feats = pl.ds(pl.multiple_of(chunk * 256, 256), 256)
            lhs = rows[:, :, :, :, :CAP, feats].reshape(1024, 256).T
            for n in range(2):
                emit(c, n, dot(lhs, pregrad[:, n * 512 : n * 512 + 512], 1, 0))

    def down_part(half, n0, emit):
        blocks = (block(n0), block(n0 + 1))
        lhs = jnp.concatenate(
            [
                hidden[:, pl.ds(pl.multiple_of(half * 512 + k * LANES, LANES), LANES)].T
                for k in blocks
            ],
            axis=0,
        )
        for n in range(2):
            rhs = rows[:, :, :, :, CAP:, n * 512 : n * 512 + 512].reshape(1024, 512)
            v = dot(lhs, rhs, 1, 0)
            emit(blocks[0], n, v[:LANES])
            emit(blocks[1], n, v[LANES:])

    def ysend(t, k):
        src, dst = ((su_out, su_in), (sd_out, sd_in))[t]
        return pltpu.make_async_remote_copy(
            src_ref=src.at[k], dst_ref=dst.at[k],
            send_sem=ys_sem.at[t, k], recv_sem=yr_sem.at[t, k],
            device_id=twin, device_id_type=MESH,
        )

    def emit_up_out(c, n, v):
        for k in range(4):
            su_out[k, c, :, (1 - n) * 512 : (2 - n) * 512] = v[64 * k : 64 * k + 64].astype(BF)

    def emit_up_own(c, n, v):
        for k in range(4):
            pu[k, c, :, n * 512 : n * 512 + 512] = v[64 * k : 64 * k + 64]

    def emit_down_out(k, n, v):
        sd_out[k, :, n * 512 : n * 512 + 512] = v.astype(BF)

    def emit_down_own(k, n, v):
        pd[k, :, n * 512 : n * 512 + 512] = v

    zrefs = ((zu, zlu, zru), (zd, zld, zrd))

    def zright(t, k):
        src, dst, _ = zrefs[t]
        return pltpu.make_async_remote_copy(
            src_ref=src.at[k], dst_ref=dst.at[k],
            send_sem=zs_sem.at[t, k], recv_sem=zl_sem.at[t, k],
            device_id=right, device_id_type=MESH,
        )

    def zleft(t, k):
        src, _, dst = zrefs[t]
        return pltpu.make_async_remote_copy(
            src_ref=src.at[k], dst_ref=dst.at[k],
            send_sem=zs_sem.at[t, k], recv_sem=zr_sem.at[t, k],
            device_id=left, device_id_type=MESH,
        )

    def line(t, k, total, final):
        out, from_left, from_right = zrefs[t]

        @pl.when(zl == k)
        def _():
            final[...] = total[...]

        @pl.when((zl < k) & (zl == 0))
        def _():
            out[k] = total[...].astype(BF)

        @pl.when((zl < k) & (zl > 0))
        def _():
            zright(t, k).wait_recv()
            out[k] = (total[...] + from_left[k].astype(F32)).astype(BF)

        @pl.when(zl < k)
        def _():
            zright(t, k).start()

        @pl.when((zl > k) & (zl == NZ - 1))
        def _():
            out[k] = total[...].astype(BF)

        @pl.when((zl > k) & (zl < NZ - 1))
        def _():
            zleft(t, k).wait_recv()
            out[k] = (total[...] + from_right[k].astype(F32)).astype(BF)

        @pl.when(zl > k)
        def _():
            zleft(t, k).start()

    def step(t, n):
        k = block(n)
        own, came = ((pu, su_in), (pd, sd_in))[t]
        ysend(t, k).wait_recv()
        own[k] = own[k] + came[k].astype(F32)
        line(t, k, own.at[k], (fu, fd)[t])

    edge = (zl == 0) | (zl == NZ - 1)

    up_part(yf, yd, emit_up_out)
    for n in range(4):
        ysend(0, block(n)).start()
    up_part(y, yr, emit_up_own)

    @pl.when(edge)
    def _():
        step(0, 0)

    finish(*last)
    for pair in (0, 2):
        down_part(1, pair, emit_down_out)
        for n in range(pair, pair + 2):
            ysend(1, block(n)).start()

    @pl.when(jnp.logical_not(edge))
    def _():
        step(0, 0)

    down_part(0, 0, emit_down_own)
    down_part(0, 2, emit_down_own)

    @pl.loop(1, 4)
    def _(n):
        step(0, n)

    for n in range(2):
        step(1, n)

    def settle(t, final):
        _, from_left, from_right = zrefs[t]

        @pl.when(zl > 0)
        def _():
            zright(t, zl).wait_recv()
            final[...] = final[...] + from_left[zl].astype(F32)

        @pl.when(zl < NZ - 1)
        def _():
            zleft(t, zl).wait_recv()
            final[...] = final[...] + from_right[zl].astype(F32)

    settle(0, fu)
    swap = pltpu.make_async_remote_copy(
        src_ref=fu.at[1], dst_ref=xu,
        send_sem=xs_sem.at[0], recv_sem=xr_sem.at[0],
        device_id=mate, device_id_type=MESH,
    )
    swap.start()
    for n in range(2, 4):
        step(1, n)

    for h, i in pairs:
        give_back(h, i).wait_recv()
        give_gate(h, i).wait_recv()
    spread = jnp.where(iota((TOK, 512), 1).astype(F32) == slot_col, 1.0, 0.0).astype(BF)

    @pl.loop(0, D // 512)
    def _(n):
        cols = pl.ds(pl.multiple_of(n * 512, 512), 512)
        tg_ref[:, cols] = dot(spread, back[:, :, :, cols].reshape(512, 512), 1, 0).astype(BF)

    lane = iota((TOK, LANES), 1).astype(F32)
    gate_sum = jnp.zeros((TOK, LANES), F32)
    for h in range(2):
        for i in range(8):
            base = float(h * 256 + i * CAP)
            hit = (lane < float(CAP)) & (lane + base == slot_col)
            gate_sum += jnp.where(hit, ggback[h, i, 0:1, :], 0.0)
    gate_total = jnp.sum(gate_sum, axis=1, keepdims=True) / gate_col
    eye = iota((TOK, TOK), 0) == iota((TOK, TOK), 1)
    gg_ref[...] = jnp.sum(jnp.where(eye, gate_total, 0.0), axis=0, keepdims=True).astype(BF)

    scale = 1.0 / (NY * NZ)

    def ff_chunk(c):
        return pl.ds(pl.multiple_of(c * 512, 512), 512)

    swap.wait_recv()
    ug_ref[:, ff_chunk(y)] = fu[0, :, 0:512] * scale
    ug_ref[:, ff_chunk(yf)] = fu[0, :, 512:1024] * scale
    ug_ref[:, ff_chunk(yr)] = xu[:, 0:512] * scale
    ug_ref[:, ff_chunk(yd)] = xu[:, 512:1024] * scale
    settle(1, fd)
    dg_ref[...] = fd[...] * scale

    swap.wait_send()
    relay(0, 0).wait_send()
    for h, i in pairs:
        dispatch(h, i).wait_send()
        relay(h, i).wait_send()
        give_back(h, i).wait_send()
        give_gate(h, i).wait_send()
    for h in range(2):
        for q in range(2):
            share_fg(h, q).wait_send()
            share_gate(h, q).wait_send()

    @pl.loop(0, 4)
    def _(k):
        ysend(0, k).wait_send()
        ysend(1, k).wait_send()

        @pl.when(zl != k)
        def _():
            zright(0, k).wait_send()
            zright(1, k).wait_send()


def tail(tg_in, gg_in, ug_in, dg_in, tg_out, gg_out, ug_out, dg_out, sem):
    moves = ((tg_in, tg_out), (ug_in, ug_out), (dg_in, dg_out))
    copies = [pltpu.make_async_copy(a, b, sem.at[n]) for n, (a, b) in enumerate(moves)]
    for copy in copies:
        copy.start()
    gg_out[...] = gg_in[...].reshape(TOK)
    for copy in copies:
        copy.wait()


def per_device(tokens, out_grad, gate_prob, expert_id, up_weight, down_weight):
    any_spec = pl.BlockSpec(memory_space=pl.ANY)
    vmem = pl.BlockSpec(memory_space=pltpu.VMEM)
    up_blocks = pltpu.VMEM((4, 2, 64, 1024), BF)
    down_blocks = pltpu.VMEM((4, 128, D), BF)
    grads = pltpu.VMEM((2, 8, CAP, D), BF)
    gates = pltpu.VMEM((2, 8, 8, LANES), F32)
    dma = pltpu.SemaphoreType.DMA
    tg, gg, ug, dg = pl.pallas_call(
        kernel,
        out_shape=(
            jax.ShapeDtypeStruct((TOK, D), BF),
            jax.ShapeDtypeStruct((1, TOK), BF),
            jax.ShapeDtypeStruct((64, FF), F32),
            jax.ShapeDtypeStruct((128, D), F32),
        ),
        in_specs=[any_spec] * 6,
        out_specs=(vmem, vmem, vmem, vmem),
        scratch_shapes=[
            pltpu.VMEM((TOK,), BF),
            pltpu.VMEM((1, TOK), jnp.int32),
            pltpu.VMEM((TOK, D), BF),
            pltpu.VMEM((TOK, D), BF),
            pltpu.VMEM((D, 1024), BF),
            pltpu.VMEM((1024, D), BF),
            pltpu.VMEM((2, 8, 2 * CAP, D), BF),
            pltpu.VMEM((2, 4, 2, 2, 2 * CAP, D), BF),
            pltpu.VMEM((1024, 1024), BF),
            pltpu.VMEM((1024, 1024), BF),
            grads, grads, grads, grads,
            gates, gates, gates, gates, gates,
            up_blocks, down_blocks, up_blocks, down_blocks, up_blocks, down_blocks,
            up_blocks, down_blocks, up_blocks, down_blocks,
            pltpu.VMEM((2, 64, 1024), F32),
            pltpu.VMEM((128, D), F32),
            pltpu.VMEM((64, 1024), F32),
            pltpu.VMEM((4, 2, 64, 1024), F32),
            pltpu.VMEM((4, 128, D), F32),
            dma((8,)),
            dma((2, 8)), dma((2, 8)), dma((2, 8)), dma((2, 8)),
            dma((2, 2)), dma((2, 2)), dma((2, 2)), dma((2, 2)),
            dma((2, 8)), dma((2, 8)), dma((2, 8)), dma((2, 8)),
            dma((2, 4)), dma((2, 4)), dma((2, 4)), dma((2, 4)), dma((2, 4)), dma((1,)), dma((1,)),
        ],
        compiler_params=pltpu.CompilerParams(
            collective_id=0, has_side_effects=True, vmem_limit_bytes=52 * 1024 * 1024
        ),
    )(
        *(
            pltpu.with_memory_space_constraint(x, pltpu.HBM)
            for x in (tokens, out_grad, gate_prob, expert_id.reshape(1, TOK))
        ),
        up_weight[0],
        down_weight[0],
    )
    tg, gg, ug, dg = pl.pallas_call(
        tail,
        out_shape=(
            jax.ShapeDtypeStruct((TOK, D), BF),
            jax.ShapeDtypeStruct((TOK,), BF),
            jax.ShapeDtypeStruct((64, FF), F32),
            jax.ShapeDtypeStruct((128, D), F32),
        ),
        in_specs=[vmem, vmem, vmem, vmem],
        out_specs=(any_spec, vmem, any_spec, any_spec),
        scratch_shapes=[
            dma((3,)),
        ],
        compiler_params=pltpu.CompilerParams(vmem_limit_bytes=2 * 1024 * 1024),
    )(tg, gg, ug, dg)
    return tg, gg, ug[None], dg[None]


def solution(mesh):
    return jax.shard_map(
        per_device,
        mesh=mesh,
        in_specs=(
            P(("dp", "expert"), None),
            P(("dp", "expert"), None),
            P(("dp", "expert")),
            P(("dp", "expert")),
            P("expert", None, None),
            P("expert", None, None),
        ),
        out_specs=(
            P(("dp", "expert"), None),
            P(("dp", "expert")),
            P("expert", "dp", None),
            P("expert", "dp", None),
        ),
        check_vma=False,
    )
```
